32 devices in a mesh: fiber: 8 (over z, core), group: 4 (over y, x).
Axes of the slice: x: 2, y: 2, z: 4, core: 2. Of those that a mesh axis runs over, the one named last changes fastest.
Arguments:
- field_slab: float32 [512, 64, 2048], P('fiber', 'group'), may hold values from -42 to 42
- start_basis: float32 [512, 128], replicated, may hold values from -6 to 6
Outputs:
- factor: float32 [512, 128], replicated
- core_slab: float32 [128, 64, 2048], P(None, 'group', 'fiber')
The draws below stay inside these ranges and needn't reach their ends.
All inputs are finite; a program needn't handle non-finite values.
Results may differ from the reference program's by a relative error of at most 0.0003.
Values sent between devices are 32-bit elements; how exact they have to be, the bound alone decides.
No kernel may reach another device: no remote copies, remote signals or barrier semaphores. Data moves between devices by JAX's collectives and lax.ppermute only.
A program may use at most 128 MiB of HBM per device.

```python
import math
import jax
import jax.numpy as jnp
from jax import lax

MODE = 512
RANK = 128
FIB_COLS = 256
ITERS = 2
BLOCKS = 64
WIDTH = 2048


def draw_field_slab(key, part):
    keys = jax.random.split(jax.random.fold_in(key, 7), 4)
    segments = WIDTH // FIB_COLS
    mode_pos = jnp.arange(MODE, dtype=jnp.float32)
    decay = jnp.exp(-math.log(100.0) * mode_pos / MODE)
    energy = jnp.mean(decay * decay)
    mixing = jax.random.uniform(keys[0], (MODE, MODE), jnp.float32, -math.sqrt(3.0), math.sqrt(3.0))
    mixing = mixing * (decay / jnp.sqrt(MODE * energy))[None, :]
    row_scale = jnp.exp(jax.random.uniform(keys[1], (MODE, 1, 1, 1), jnp.float32, math.log(0.5), math.log(2.0)))
    block_scale = jnp.exp(jax.random.uniform(keys[2], (MODE, BLOCKS, segments, 1), jnp.float32, math.log(0.3), math.log(3.0)))

    def one_block(index):
        pair = jax.random.split(jax.random.fold_in(keys[3], index), 2)
        latent = jax.random.truncated_normal(pair[0], -4.0, 4.0, (MODE, WIDTH), jnp.float32)
        noise = jax.random.truncated_normal(pair[1], -4.0, 4.0, (MODE, WIDTH), jnp.float32)
        mixed = jnp.dot(mixing, latent, precision=lax.Precision.HIGHEST) + 0.2 * noise
        return jnp.clip(mixed, -4.0, 4.0)
    stacked = lax.map(one_block, jnp.arange(BLOCKS))
    base = jnp.moveaxis(stacked, 0, 1).reshape(MODE, BLOCKS, segments, FIB_COLS)
    order = jnp.arange(segments, dtype=jnp.float32)[None, :] * BLOCKS + jnp.arange(BLOCKS, dtype=jnp.float32)[:, None]
    ramp = 1.0 + 0.75 * order / (BLOCKS * segments)
    values = base * row_scale * block_scale * ramp[None, :, :, None]
    return values.reshape(MODE, BLOCKS, WIDTH).astype(jnp.float32)


def centred(own_key, shape, spread, limit, held_as=jnp.bfloat16):
    result = jax.random.normal(own_key, shape, jnp.float32) * spread
    return jnp.minimum(jnp.maximum(result, -limit), limit).astype(held_as)


def setup_inputs(seed: int = 0) -> dict:
    arg_keys = jax.random.split(jax.random.key(seed), 3)
    field_slab = draw_field_slab(jax.random.fold_in(arg_keys[2], 71), 0)
    start_basis = centred(arg_keys[1], (MODE, RANK), 1.0, 6.0, jnp.float32)
    return dict(field_slab=field_slab, start_basis=start_basis)


precise = lax.Precision.HIGHEST

def orthonormal(images):
    inner_products = jnp.dot(images.T, images, precision=precise)
    cholesky_factor = jnp.linalg.cholesky(inner_products)
    return lax.linalg.triangular_solve(cholesky_factor, images, left_side=False, lower=True, transpose_a=True)

def reference(field_slab, start_basis):
    unfolded = field_slab.reshape(MODE, BLOCKS * WIDTH)
    gram_matrix = jnp.dot(unfolded, unfolded.T, precision=precise) / (BLOCKS * WIDTH)
    subspace = start_basis
    for iteration in range(ITERS):
        subspace = orthonormal(jnp.dot(gram_matrix, subspace, precision=precise))
    core_slab = jnp.einsum('mk,mbw->kbw', subspace, field_slab, precision=precise)
    return (subspace, core_slab)
```

```python
import functools

import jax
import jax.numpy as jnp
from jax import lax
from jax.experimental import pallas as pl
from jax.experimental.pallas import tpu as pltpu
from jax.sharding import PartitionSpec as P

ITERS = 2
LANES = 128
ROWS = 8


precise = lax.Precision.HIGHEST
VMEM = pl.BlockSpec(memory_space=pltpu.VMEM)


def contract_lanes(left, right):
    return lax.dot_general(left, right, (((1,), (1,)), ((), ())), preferred_element_type=jnp.float32)


def matmul(left, right):
    return lax.dot_general(left, right, (((1,), (0,)), ((), ())), preferred_element_type=jnp.float32)


def split(values):
    high = values.astype(jnp.bfloat16)
    low = (values - high.astype(jnp.float32)).astype(jnp.bfloat16)
    return high, low


def pack_kernel(targets, field_ref, *piece_refs):
    for k, piece_ref in enumerate(piece_refs):

        @pl.when(pl.program_id(0) == k)
        def _():
            for block in range(ROWS):
                piece_ref[block] = field_ref[:, block, :]


def pack(field_slab, targets, block_part, lane_part):
    fibers = targets.shape[0]
    mode_rows, _, width = field_slab.shape
    lane_parts = width // fibers // LANES
    piece = (ROWS, mode_rows, LANES)
    return pl.pallas_call(
        pack_kernel,
        out_shape=[jax.ShapeDtypeStruct(piece, jnp.float32)] * fibers,
        grid_spec=pltpu.PrefetchScalarGridSpec(
            num_scalar_prefetch=1,
            grid=(fibers,),
            in_specs=[
                pl.BlockSpec(
                    (mode_rows, ROWS, LANES),
                    lambda k, targets: (0, block_part, targets[k] * lane_parts + lane_part),
                )
            ],
            out_specs=[pl.BlockSpec(piece, lambda k, targets: (0, 0, 0))] * fibers,
        ),
        cost_estimate=pl.CostEstimate(flops=0, bytes_accessed=2 * fibers * 4 * ROWS * mode_rows * LANES, transcendentals=0),
        name="pack",
    )(targets, field_slab)


def gram_kernel(fibers, sources, *refs):
    pieces = refs[:fibers]
    sum_in, high_ref, low_ref, sum_ref = refs[fibers:]
    mode_rows = pieces[0].shape[1]
    for k, piece in enumerate(pieces):
        rows = pl.ds(pl.multiple_of(sources[k] * mode_rows, mode_rows), mode_rows)
        for block in range(ROWS):
            high, low = split(piece[block])
            columns = slice(block * LANES, (block + 1) * LANES)
            high_ref[rows, columns] = high
            low_ref[rows, columns] = low
    mode = high_ref.shape[0]
    place = 0
    step = 2 * LANES
    for top in range(0, mode, step):
        high, low = high_ref[top : top + step], low_ref[top : top + step]
        products = (
            contract_lanes(high, high_ref[top:])
            + contract_lanes(high, low_ref[top:])
            + contract_lanes(low, high_ref[top:])
        )
        for row in range(0, step, LANES):
            for column in range(row, mode - top, LANES):
                target = slice(place, place + LANES)
                sum_ref[target] = sum_in[target] + products[row : row + LANES, column : column + LANES]
                place += LANES


def gram(sources, pieces, running):
    fibers = len(pieces)
    mode = fibers * pieces[0].shape[1]
    columns = ROWS * LANES
    half = jax.ShapeDtypeStruct((mode, columns), jnp.bfloat16)
    return pl.pallas_call(
        functools.partial(gram_kernel, fibers),
        out_shape=[half, half, jax.ShapeDtypeStruct(running.shape, jnp.float32)],
        in_specs=[pl.BlockSpec(memory_space=pltpu.SMEM)] + [VMEM] * (fibers + 1),
        out_specs=[VMEM] * 3,
        input_output_aliases={fibers + 1: 2},
        cost_estimate=pl.CostEstimate(flops=6 * mode * mode * columns, bytes_accessed=8 * mode * columns, transcendentals=0),
        name="gram",
    )(sources, *pieces, running)


def core_kernel(parts, lane_parts, basis_ref, *refs):
    core_ref = refs[-1]
    high, low = split(basis_ref[...])
    rank = high.shape[0]
    both = jnp.concatenate([high, low], axis=0)
    for part in range(parts):
        block_part, lane_part = divmod(part, lane_parts)
        field_high, field_low = refs[2 * part], refs[2 * part + 1]
        products = matmul(both, field_high[...])
        result = products[:rank] + products[rank:] + matmul(high, field_low[...])
        for block in range(ROWS):
            core_ref[:, block_part * ROWS + block, lane_part * LANES : (lane_part + 1) * LANES] = result[
                :, block * LANES : (block + 1) * LANES
            ]


def core_product(basis_rows, halves, blocks, width):
    rank = basis_rows.shape[0]
    parts = len(halves) // 2
    return pl.pallas_call(
        functools.partial(core_kernel, parts, width // LANES),
        out_shape=jax.ShapeDtypeStruct((rank, blocks, width), jnp.float32),
        in_specs=[VMEM] * (1 + len(halves)),
        out_specs=VMEM,
        name="core",
    )(basis_rows, *halves)


def orthonormal(images):
    inner_products = jnp.dot(images.T, images, precision=precise)
    cholesky_factor = jnp.linalg.cholesky(inner_products)
    return lax.linalg.triangular_solve(
        cholesky_factor, images, left_side=False, lower=True, transpose_a=True
    )


def unpack_symmetric(packed, mode):
    count = mode // LANES
    tiles, place = {}, 0
    for i in range(count):
        for j in range(i, count):
            tile = packed[place : place + LANES]
            tiles[i, j], tiles[j, i] = tile, tile.T
            place += LANES
    return jnp.concatenate(
        [jnp.concatenate([tiles[i, j] for j in range(count)], axis=1) for i in range(count)], axis=0
    )


def on_device(field_slab, start_basis):
    fibers, groups = lax.axis_size("fiber"), lax.axis_size("group")
    mode_rows, blocks, width = field_slab.shape
    mode = fibers * mode_rows
    column_count = blocks * width * groups
    own_width = width // fibers
    me = lax.axis_index("fiber")
    shifts = sorted(range(fibers), key=lambda shift: (abs(shift - fibers // 2), shift))
    targets = lax.rem(me + jnp.array(shifts, jnp.int32), jnp.int32(fibers))
    sources = lax.rem(me + fibers - jnp.array(shifts, jnp.int32), jnp.int32(fibers))
    count = mode // LANES
    running = jnp.zeros((count * (count + 1) // 2 * LANES, LANES), jnp.float32)
    halves = []
    for block_part in range(blocks // ROWS):
        for lane_part in range(own_width // LANES):
            pieces = pack(field_slab, targets, block_part, lane_part)
            arrived = [
                piece
                if shift == 0
                else lax.ppermute(piece, "fiber", [(i, (i + shift) % fibers) for i in range(fibers)])
                for piece, shift in zip(pieces, shifts)
            ]
            high, low, running = gram(sources, arrived, running)
            halves += [high, low]
    devices = fibers * groups
    everywhere = ("fiber", "group")
    shares = lax.all_to_all(running.reshape(devices, -1, LANES), everywhere, 0, 0)
    share = jnp.sum(shares, axis=0) / column_count
    packed = lax.all_to_all(jnp.broadcast_to(share, (devices,) + share.shape), everywhere, 0, 0)
    gram_matrix = unpack_symmetric(packed.reshape(running.shape), mode)
    subspace = start_basis
    for iteration in range(ITERS):
        subspace = orthonormal(jnp.dot(gram_matrix, subspace, precision=precise))
    core_slab = core_product(subspace.T, halves, blocks, own_width)
    return (subspace, core_slab)


def solution(mesh):
    return jax.shard_map(
        on_device,
        mesh=mesh,
        in_specs=(P("fiber", "group", None), P()),
        out_specs=(P(), P(None, "group", "fiber")),
        check_vma=False,
    )
```

```python
import functools

import jax
import jax.numpy as jnp
from jax import lax
from jax.experimental import pallas as pl
from jax.experimental.pallas import tpu as pltpu
from jax.sharding import PartitionSpec as P

ITERS = 2
LANES = 128
ROWS = 8


precise = lax.Precision.HIGHEST
VMEM = pl.BlockSpec(memory_space=pltpu.VMEM)


def contract_lanes(left, right):
    return lax.dot_general(left, right, (((1,), (1,)), ((), ())), preferred_element_type=jnp.float32)


def matmul(left, right):
    return lax.dot_general(left, right, (((1,), (0,)), ((), ())), preferred_element_type=jnp.float32)


def split(values):
    high = values.astype(jnp.bfloat16)
    low = (values - high.astype(jnp.float32)).astype(jnp.bfloat16)
    return high, low


def shift_of(place, fibers):
    half = (place + 1) // 2
    return fibers // 2 + half - (place % 2) * 2 * half


def pack_kernel(me, field_ref, *piece_refs):
    for step, piece_ref in enumerate(piece_refs):

        @pl.when(pl.program_id(0) == step)
        def _():
            for block in range(ROWS):
                piece_ref[block] = field_ref[:, block, :]


def pack(field_slab, me, fibers, part, first, last):
    mode_rows, _, width = field_slab.shape
    lane_parts = width // fibers // LANES
    block_part, lane_part = divmod(part, lane_parts)
    piece = (ROWS, mode_rows, LANES)

    def place(step, me):
        target = lax.rem(me[0] + shift_of(step + first, fibers), fibers)
        return 0, block_part, target * lane_parts + lane_part

    return pl.pallas_call(
        pack_kernel,
        out_shape=[jax.ShapeDtypeStruct(piece, jnp.float32)] * (last - first),
        grid_spec=pltpu.PrefetchScalarGridSpec(
            num_scalar_prefetch=1,
            grid=(last - first,),
            in_specs=[pl.BlockSpec((mode_rows, ROWS, LANES), place)],
            out_specs=[pl.BlockSpec(piece, lambda step, me: (0, 0, 0))] * (last - first),
        ),
        cost_estimate=pl.CostEstimate(
            flops=0, bytes_accessed=8 * (last - first) * ROWS * mode_rows * LANES, transcendentals=0
        ),
        name="pack",
    )(me, field_slab)


def gram_kernel(fibers, me, *refs):
    pieces = refs[:fibers]
    sum_in, high_ref, low_ref, sum_ref = refs[fibers:]
    blocks, mode_rows = pieces[0].shape[:2]
    mode = high_ref.shape[0]
    for place, piece in enumerate(pieces):
        source = lax.rem(me[0] + fibers - shift_of(place, fibers), fibers)
        rows = pl.ds(pl.multiple_of(source * mode_rows, mode_rows), mode_rows)
        for block in range(blocks):
            high, low = split(piece[block])
            columns = slice(block * LANES, (block + 1) * LANES)
            high_ref[rows, columns] = high
            low_ref[rows, columns] = low

    @pl.when(pl.program_id(0) == 0)
    def _():
        sum_ref[...] = sum_in[...]

    place = 0
    step = 2 * LANES
    for top in range(0, mode, step):
        high, low = high_ref[top : top + step], low_ref[top : top + step]
        products = (
            contract_lanes(high, high_ref[top:])
            + contract_lanes(high, low_ref[top:])
            + contract_lanes(low, high_ref[top:])
        )
        for row in range(0, step, LANES):
            for column in range(row, mode - top, LANES):
                sum_ref[place : place + LANES] += products[row : row + LANES, column : column + LANES]
                place += LANES


def gram(me, pieces, running):
    fibers = len(pieces)
    mode = fibers * pieces[0].shape[1]
    columns = ROWS * LANES
    blocks = 2
    half = jax.ShapeDtypeStruct((mode, columns), jnp.bfloat16)
    half_spec = pl.BlockSpec((mode, blocks * LANES), lambda step, me: (0, step))
    sum_spec = pl.BlockSpec(running.shape, lambda step, me: (0, 0))
    piece_spec = pl.BlockSpec((blocks,) + pieces[0].shape[1:], lambda step, me: (step, 0, 0))
    return pl.pallas_call(
        functools.partial(gram_kernel, fibers),
        out_shape=[half, half, jax.ShapeDtypeStruct(running.shape, jnp.float32)],
        grid_spec=pltpu.PrefetchScalarGridSpec(
            num_scalar_prefetch=1,
            grid=(ROWS // blocks,),
            in_specs=[piece_spec] * fibers + [sum_spec],
            out_specs=[half_spec, half_spec, sum_spec],
        ),
        input_output_aliases={fibers + 1: 2},
        cost_estimate=pl.CostEstimate(flops=6 * mode * mode * columns, bytes_accessed=8 * mode * columns, transcendentals=0),
        name="gram",
    )(me, *pieces, running)


def dot(left, right, left_dim, right_dim):
    return lax.dot_general(
        left, right, (((left_dim,), (right_dim,)), ((), ())), precision=precise, preferred_element_type=jnp.float32
    )


def inverse_cholesky(inner, panel=32):
    rank = inner.shape[0]
    row = lax.broadcasted_iota(jnp.int32, (ROWS, 1), 0)
    rows = lax.broadcasted_iota(jnp.int32, (rank, rank), 0)
    lanes = lax.broadcasted_iota(jnp.int32, (rank, rank), 1)
    inverse = (rows == lanes).astype(jnp.float32)
    done = []
    for start in range(0, rank, panel):
        groups = panel // ROWS
        left = [inner[ROWS * i : ROWS * (i + 1)] for i in range(groups)]
        right = [inverse[ROWS * i : ROWS * (i + 1)] for i in range(groups)]
        for j in range(panel):
            group, sub = divmod(j, ROWS)
            column = slice(start + j, start + j + 1)
            left_row, right_row = left[group][sub : sub + 1], right[group][sub : sub + 1]
            pivot = 1.0 / left_row[:, column]
            left_row, right_row = left_row * pivot, right_row * pivot
            for i in range(group, groups):
                scale = left[i][:, column]
                if i == group:
                    if sub == ROWS - 1:
                        continue
                    scale = jnp.where(row > sub, scale, 0.0)
                left[i] = left[i] - scale * left_row
                right[i] = right[i] - scale * right_row
        left, right = jnp.concatenate(left, axis=0), jnp.concatenate(right, axis=0)
        diagonal = jnp.where(lanes[:panel] == rows[:panel] + start, left, 0.0)
        root = lax.rsqrt(jnp.sum(diagonal, axis=1, keepdims=True))
        left, right = left * root, right * root
        done.append(right)
        end = start + panel
        if end < rank:
            update = dot(left, jnp.concatenate([left, right], axis=1), 0, 0)
            inner = inner[panel:] - update[end:, :rank]
            inverse = inverse[panel:] - update[end:, rank:]
    return jnp.concatenate(done, axis=0)


def finish_kernel(parts, lane_parts, packed_ref, start_ref, *refs):
    halves, refs = refs[: 2 * parts], refs[2 * parts :]
    factor_ref, core_ref, gram_ref, field_ref, result_ref, in_sem, out_sem = refs
    loads = [pltpu.make_async_copy(half, field_ref.at[i], in_sem.at[i]) for i, half in enumerate(halves)]
    for load in loads:
        load.start()
    mode, rank = start_ref.shape
    place = 0
    for i in range(0, mode, LANES):
        for j in range(i, mode, LANES):
            tile = packed_ref[place : place + LANES]
            gram_ref[i : i + LANES, j : j + LANES] = tile
            if j > i:
                gram_ref[j : j + LANES, i : i + LANES] = tile.T
            place += LANES
    basis = start_ref[...].T
    for iteration in range(ITERS):
        images = dot(basis, gram_ref[...], 1, 0)
        basis = dot(inverse_cholesky(dot(images, images, 1, 1)), images, 1, 0)
    factor_ref[...] = basis.T
    high, low = split(basis)
    both = jnp.concatenate([high, low], axis=0)
    stores = []
    for part in range(parts):
        loads[2 * part].wait()
        loads[2 * part + 1].wait()
        products = matmul(both, field_ref[2 * part])
        result = products[:rank] + products[rank:] + matmul(high, field_ref[2 * part + 1])
        for block in range(ROWS):
            result_ref[part, :, block, :] = result[:, block * LANES : (block + 1) * LANES]
        block_part, lane_part = divmod(part, lane_parts)
        rows, lanes = pl.ds(block_part * ROWS, ROWS), pl.ds(lane_part * LANES, LANES)
        stores.append(pltpu.make_async_copy(result_ref.at[part], core_ref.at[:, rows, lanes], out_sem.at[part]))
        stores[-1].start()
    for store in stores:
        store.wait()


def finish(packed, start_basis, halves, blocks, width):
    mode, rank = start_basis.shape
    parts = len(halves) // 2
    anywhere = pl.BlockSpec(memory_space=pl.ANY)
    return pl.pallas_call(
        functools.partial(finish_kernel, parts, width // LANES),
        out_shape=[
            jax.ShapeDtypeStruct((mode, rank), jnp.float32),
            jax.ShapeDtypeStruct((rank, blocks, width), jnp.float32),
        ],
        in_specs=[VMEM, VMEM] + [anywhere] * len(halves),
        out_specs=[VMEM, anywhere],
        scratch_shapes=[
            pltpu.VMEM((mode, mode), jnp.float32),
            pltpu.VMEM((len(halves),) + halves[0].shape, jnp.bfloat16),
            pltpu.VMEM((parts, rank, ROWS, LANES), jnp.float32),
            pltpu.SemaphoreType.DMA((len(halves),)),
            pltpu.SemaphoreType.DMA((parts,)),
        ],
        name="finish",
    )(packed, start_basis, *halves)


def on_device(field_slab, start_basis):
    fibers, groups = lax.axis_size("fiber"), lax.axis_size("group")
    mode_rows, blocks, width = field_slab.shape
    mode = fibers * mode_rows
    column_count = blocks * width * groups
    own_width = width // fibers
    me = lax.axis_index("fiber").reshape(1)
    count = mode // LANES
    running = jnp.zeros((count * (count + 1) // 2 * LANES, LANES), jnp.float32)
    halves = []
    for part in range(blocks // ROWS * (own_width // LANES)):
        if part == 0:
            pieces = [*pack(field_slab, me, fibers, part, 0, 1), *pack(field_slab, me, fibers, part, 1, fibers)]
        else:
            pieces = [*pack(field_slab, me, fibers, part, 0, fibers)]
        for place in range(fibers - 1):
            shift = shift_of(place, fibers)
            ring = [(i, (i + shift) % fibers) for i in range(fibers)]
            pieces[place] = lax.ppermute(pieces[place], "fiber", ring)
        high, low, running = gram(me, pieces, running)
        halves += [high, low]
    devices = fibers * groups
    everywhere = ("fiber", "group")
    shares = lax.all_to_all(running.reshape(devices, -1, LANES), everywhere, 0, 0)
    share = jnp.sum(shares, axis=0) / column_count
    packed = lax.all_to_all(jnp.broadcast_to(share, (devices,) + share.shape), everywhere, 0, 0)
    return tuple(finish(packed.reshape(running.shape), start_basis, halves, blocks, own_width))


def solution(mesh):
    return jax.shard_map(
        on_device,
        mesh=mesh,
        in_specs=(P("fiber", "group", None), P()),
        out_specs=(P(), P(None, "group", "fiber")),
        check_vma=False,
    )
```

```python
import functools

import jax
import jax.numpy as jnp
from jax import lax
from jax.experimental import pallas as pl
from jax.experimental.pallas import tpu as pltpu
from jax.sharding import PartitionSpec as P

ITERS = 2
LANES = 128
ROWS = 8


precise = lax.Precision.HIGHEST
VMEM = pl.BlockSpec(memory_space=pltpu.VMEM)


def contract_lanes(left, right):
    return lax.dot_general(left, right, (((1,), (1,)), ((), ())), preferred_element_type=jnp.float32)


def matmul(left, right):
    return lax.dot_general(left, right, (((1,), (0,)), ((), ())), preferred_element_type=jnp.float32)


def split(values):
    high = values.astype(jnp.bfloat16)
    low = (values - high.astype(jnp.float32)).astype(jnp.bfloat16)
    return high, low


def shift_of(place, fibers):
    half = (place + 1) // 2
    return fibers // 2 + half - (place % 2) * 2 * half


def pack_kernel(start, me, field_ref, *piece_refs):
    for step, piece_ref in enumerate(piece_refs):

        @pl.when(pl.program_id(0) == step)
        def _():
            for block in range(piece_ref.shape[0]):
                piece_ref[block] = field_ref[:, start % ROWS + block, :]


def pack(field_slab, me, fibers, part, first, last):
    mode_rows, _, width = field_slab.shape
    lane_parts = width // fibers // LANES
    start, count, lane_part = part
    block_part = start // ROWS
    piece = (count, mode_rows, LANES)

    def place(step, me):
        target = lax.rem(me[0] + shift_of(step + first, fibers), fibers)
        return 0, block_part, target * lane_parts + lane_part

    return pl.pallas_call(
        functools.partial(pack_kernel, start),
        out_shape=[jax.ShapeDtypeStruct(piece, jnp.float32)] * (last - first),
        grid_spec=pltpu.PrefetchScalarGridSpec(
            num_scalar_prefetch=1,
            grid=(last - first,),
            in_specs=[pl.BlockSpec((mode_rows, ROWS, LANES), place)],
            out_specs=[pl.BlockSpec(piece, lambda step, me: (0, 0, 0))] * (last - first),
        ),
        cost_estimate=pl.CostEstimate(
            flops=0, bytes_accessed=8 * (last - first) * count * mode_rows * LANES, transcendentals=0
        ),
        name="pack",
    )(me, field_slab)


def gram_kernel(fibers, last, me, *refs):
    pieces = refs[:fibers]
    sum_in, high_ref, low_ref, *sum_refs = refs[fibers:]
    blocks, mode_rows = pieces[0].shape[:2]
    mode = high_ref.shape[0]
    for place, piece in enumerate(pieces):
        source = lax.rem(me[0] + fibers - shift_of(place, fibers), fibers)
        rows = pl.ds(pl.multiple_of(source * mode_rows, mode_rows), mode_rows)
        for block in range(blocks):
            high, low = split(piece[block])
            columns = slice(block * LANES, (block + 1) * LANES)
            high_ref[rows, columns] = high
            low_ref[rows, columns] = low
    half = sum_in.shape[0] // 2
    place = 0
    step = 2 * LANES
    for top in range(0, mode, step):
        high, low = high_ref[top : top + step], low_ref[top : top + step]
        products = (
            contract_lanes(high, high_ref[top:])
            + contract_lanes(high, low_ref[top:])
            + contract_lanes(low, high_ref[top:])
        )
        for row in range(0, step, LANES):
            for column in range(row, mode - top, LANES):
                tile = sum_in[place : place + LANES] + products[row : row + LANES, column : column + LANES]
                if last:
                    index, offset = divmod(place, half)
                    sum_refs[0][lax.rem(me[1] + index, 2), offset : offset + LANES] = tile
                else:
                    sum_refs[0][place : place + LANES] = tile
                place += LANES
    if last:
        ordered, own_ref, other_ref = sum_refs
        own_ref[...] = ordered[0]
        other_ref[...] = ordered[1]


def gram(me, pieces, running, last):
    fibers = len(pieces)
    blocks, mode_rows, _ = pieces[0].shape
    mode, columns = fibers * mode_rows, blocks * LANES
    half = jax.ShapeDtypeStruct((mode, columns), jnp.bfloat16)
    total, lanes = running.shape
    if last:
        sums = [jax.ShapeDtypeStruct((total // 2, lanes), jnp.float32)] * 2
        scratch, aliases = [pltpu.VMEM((2, total // 2, lanes), jnp.float32)], {}
    else:
        sums, scratch, aliases = [jax.ShapeDtypeStruct(running.shape, jnp.float32)], [], {fibers + 1: 2}

    def kernel(*refs):
        if last:
            *refs, own_ref, other_ref, ordered = refs
            refs += [ordered, own_ref, other_ref]
        gram_kernel(fibers, last, *refs)

    return pl.pallas_call(
        kernel,
        out_shape=[half, half] + sums,
        in_specs=[pl.BlockSpec(memory_space=pltpu.SMEM)] + [VMEM] * (fibers + 1),
        out_specs=[VMEM] * (2 + len(sums)),
        scratch_shapes=scratch,
        input_output_aliases=aliases,
        cost_estimate=pl.CostEstimate(flops=6 * mode * mode * columns, bytes_accessed=8 * mode * columns, transcendentals=0),
        name="gram",
    )(me, *pieces, running)


def dot(left, right, left_dim, right_dim):
    return lax.dot_general(
        left, right, (((left_dim,), (right_dim,)), ((), ())), precision=precise, preferred_element_type=jnp.float32
    )


def inverse_cholesky(inner, panel=32, block=16):
    rank = inner.shape[0]
    row = lax.broadcasted_iota(jnp.int32, (ROWS, rank), 0)
    rows = lax.broadcasted_iota(jnp.int32, (rank, rank), 0)
    lanes = lax.broadcasted_iota(jnp.int32, (rank, rank), 1)
    inverse = (rows == lanes).astype(jnp.float32)
    groups = panel // ROWS
    done = []
    for start in range(0, rank, panel):
        left = [inner[ROWS * i : ROWS * (i + 1)] for i in range(groups)]
        right = [inverse[ROWS * i : ROWS * (i + 1)] for i in range(groups)]
        for first in range(0, panel, block):
            columns = {}
            for i in range(first // ROWS, groups):
                for j in range(block):
                    column = left[i][:, start + first + j : start + first + j + 1]
                    columns[i, j] = jnp.broadcast_to(column, (ROWS, rank))
            for j in range(block):
                group, sub = divmod(first + j, ROWS)
                pivot_row = slice(sub, sub + 1)
                pivot = 1.0 / columns[group, j][pivot_row]
                heads = {k: columns[group, k][pivot_row] for k in range(j + 1, block)}
                left_row, right_row = left[group][pivot_row], right[group][pivot_row]
                for i in range(group, groups):
                    below = columns[i, j]
                    if i == group:
                        below = jnp.where(row > sub, below, 0.0)
                    scale = below * pivot
                    for k, head in heads.items():
                        change = (below * head) * pivot if k == j + 1 else scale * head
                        columns[i, k] = columns[i, k] - change
                    left[i] = left[i] - scale * left_row
                    right[i] = right[i] - scale * right_row
        top, bottom = jnp.concatenate(left, axis=0), jnp.concatenate(right, axis=0)
        diagonal = jnp.where(lanes[:panel] == rows[:panel] + start, top, 0.0)
        root = lax.rsqrt(jnp.sum(diagonal, axis=1, keepdims=True))
        top, bottom = top * root, bottom * root
        done.append(bottom)
        end = start + panel
        if end < rank:
            update = dot(top, jnp.concatenate([top, bottom], axis=1), 0, 0)
            inner = inner[panel:] - update[end:, :rank]
            inverse = inverse[panel:] - update[end:, rank:]
    return jnp.concatenate(done, axis=0)


def finish_kernel(parts, me, own_ref, other_ref, start_ref, *refs):
    count = len(parts)
    halves, (factor_ref, core_ref), refs = refs[: 2 * count], refs[2 * count : 2 * count + 2], refs[2 * count + 2 :]
    fields, refs = refs[: 2 * count], refs[2 * count :]
    results, (gram_ref, packed_ref, in_sem, out_sem) = refs[:count], refs[count:]
    loads = [pltpu.make_async_copy(half, field, in_sem.at[i]) for i, (half, field) in enumerate(zip(halves, fields))]
    for load in loads:
        load.start()
    packed_ref[me[1]] = own_ref[...]
    packed_ref[1 - me[1]] = other_ref[...]
    mode, rank = start_ref.shape
    half = own_ref.shape[0]
    place = 0
    for i in range(0, mode, LANES):
        for j in range(i, mode, LANES):
            index, offset = divmod(place, half)
            tile = packed_ref[index, offset : offset + LANES]
            gram_ref[i : i + LANES, j : j + LANES] = tile
            if j > i:
                gram_ref[j : j + LANES, i : i + LANES] = tile.T
            place += LANES
    basis = start_ref[...].T
    for iteration in range(ITERS):
        images = dot(basis, gram_ref[...], 1, 0)
        basis = dot(inverse_cholesky(dot(images, images, 1, 1)), images, 1, 0)
    factor_ref[...] = basis.T
    high, low = split(basis)
    both = jnp.concatenate([high, low], axis=0)
    stores = []
    for i, (start, blocks, lane_part) in enumerate(parts):
        loads[2 * i].wait()
        loads[2 * i + 1].wait()
        products = matmul(both, fields[2 * i][...])
        result = products[:rank] + products[rank:] + matmul(high, fields[2 * i + 1][...])
        for block in range(blocks):
            results[i][:, block, :] = result[:, block * LANES : (block + 1) * LANES]
        target = core_ref.at[:, pl.ds(start, blocks), pl.ds(lane_part * LANES, LANES)]
        stores.append(pltpu.make_async_copy(results[i], target, out_sem.at[i]))
        stores[-1].start()
    for store in stores:
        store.wait()


def finish(me, own, other, start_basis, halves, parts, blocks, width):
    mode, rank = start_basis.shape
    anywhere = pl.BlockSpec(memory_space=pl.ANY)
    return pl.pallas_call(
        functools.partial(finish_kernel, parts),
        out_shape=[
            jax.ShapeDtypeStruct((mode, rank), jnp.float32),
            jax.ShapeDtypeStruct((rank, blocks, width), jnp.float32),
        ],
        in_specs=[pl.BlockSpec(memory_space=pltpu.SMEM), VMEM, VMEM, VMEM] + [anywhere] * len(halves),
        out_specs=[VMEM, anywhere],
        scratch_shapes=[pltpu.VMEM(half.shape, half.dtype) for half in halves]
        + [pltpu.VMEM((rank, part[1], LANES), jnp.float32) for part in parts]
        + [
            pltpu.VMEM((mode, mode), jnp.float32),
            pltpu.VMEM((2,) + own.shape, jnp.float32),
            pltpu.SemaphoreType.DMA((len(halves),)),
            pltpu.SemaphoreType.DMA((len(parts),)),
        ],
        name="finish",
    )(me, own, other, start_basis, *halves)


def column_parts(blocks, lane_parts):
    parts = [(start, ROWS, lane) for start in range(0, blocks, ROWS) for lane in range(lane_parts)]
    start, count, lane = parts.pop()
    return parts + [(start, count // 2, lane), (start + count // 2, count - count // 2, lane)]


def on_device(field_slab, start_basis):
    fiber = ("chip", "core")
    fibers, groups = lax.axis_size(fiber), lax.axis_size("group")
    mode_rows, blocks, width = field_slab.shape
    mode = fibers * mode_rows
    column_count = blocks * width * groups
    own_width = width // fibers
    me = jnp.stack([lax.axis_index(fiber), lax.axis_index("core")]).astype(jnp.int32)
    count = mode // LANES
    sums = [jnp.zeros((count * (count + 1) // 2 * LANES, LANES), jnp.float32)]
    halves = []
    parts = column_parts(blocks, own_width // LANES)
    for part in parts:
        if part == parts[0]:
            pieces = [*pack(field_slab, me, fibers, part, 0, 1), *pack(field_slab, me, fibers, part, 1, fibers)]
        else:
            pieces = [*pack(field_slab, me, fibers, part, 0, fibers)]
        for place in range(fibers - 1):
            shift = shift_of(place, fibers)
            ring = [(i, (i + shift) % fibers) for i in range(fibers)]
            pieces[place] = lax.ppermute(pieces[place], fiber, ring)
        high, low, *sums = gram(me, pieces, sums[0], part == parts[-1])
        halves += [high, low]
    own, other = sums
    own = own + lax.ppermute(other, "core", [(0, 1), (1, 0)])
    peers = ("chip", "group")
    members = lax.axis_size(peers)
    shares = lax.all_to_all(own.reshape(members, -1, LANES), peers, 0, 0)
    share = jnp.sum(shares, axis=0) / column_count
    own = lax.all_to_all(jnp.broadcast_to(share, (members,) + share.shape), peers, 0, 0).reshape(own.shape)
    other = lax.ppermute(own, "core", [(0, 1), (1, 0)])
    return tuple(finish(me, own, other, start_basis, halves, parts, blocks, own_width))


def solution(mesh):
    devices = mesh.devices.reshape(mesh.shape["fiber"] // 2, 2, mesh.shape["group"])
    return jax.shard_map(
        on_device,
        mesh=jax.sharding.Mesh(devices, ("chip", "core", "group")),
        in_specs=(P(("chip", "core"), "group", None), P()),
        out_specs=(P(), P(None, "group", ("chip", "core"))),
        check_vma=False,
    )
```

```python
import functools

import jax
import jax.numpy as jnp
from jax import lax
from jax.experimental import pallas as pl
from jax.experimental.pallas import tpu as pltpu
from jax.sharding import PartitionSpec as P

ITERS = 2
LANES = 128
ROWS = 8


precise = lax.Precision.HIGHEST
VMEM = pl.BlockSpec(memory_space=pltpu.VMEM)


def contract_lanes(left, right):
    return lax.dot_general(left, right, (((1,), (1,)), ((), ())), preferred_element_type=jnp.float32)


def matmul(left, right):
    return lax.dot_general(left, right, (((1,), (0,)), ((), ())), preferred_element_type=jnp.float32)


def split(values):
    high = values.astype(jnp.bfloat16)
    low = (values - high.astype(jnp.float32)).astype(jnp.bfloat16)
    return high, low


def shift_of(place, fibers):
    half = (place + 1) // 2
    return fibers // 2 + half - (place % 2) * 2 * half


def pack_kernel(fibers, part, first, me, field_ref, *refs):
    *piece_refs, loaded_ref, sem = refs
    start, count, lane_part = part
    own_width = field_ref.shape[2] // fibers
    loads = []
    for step in range(len(piece_refs)):
        target = lax.rem(me[0] + shift_of(step + first, fibers), fibers)
        lanes = pl.ds(pl.multiple_of(target * own_width + lane_part * LANES, LANES), LANES)
        source = field_ref.at[:, pl.ds(start // ROWS * ROWS, ROWS), lanes]
        loads.append(pltpu.make_async_copy(source, loaded_ref.at[step], sem.at[step]))
        loads[-1].start()
    for step, piece_ref in enumerate(piece_refs):
        loads[step].wait()
        for block in range(count):
            piece_ref[block] = loaded_ref[step, :, start % ROWS + block, :]


def pack(field_slab, me, fibers, part, first, last):
    mode_rows = field_slab.shape[0]
    piece = (part[1], mode_rows, LANES)
    pieces = last - first
    return pl.pallas_call(
        functools.partial(pack_kernel, fibers, part, first),
        out_shape=[jax.ShapeDtypeStruct(piece, jnp.float32)] * pieces,
        in_specs=[pl.BlockSpec(memory_space=pltpu.SMEM), pl.BlockSpec(memory_space=pltpu.HBM)],
        out_specs=[VMEM] * pieces,
        scratch_shapes=[
            pltpu.VMEM((pieces, mode_rows, ROWS, LANES), jnp.float32),
            pltpu.SemaphoreType.DMA((pieces,)),
        ],
        cost_estimate=pl.CostEstimate(
            flops=0, bytes_accessed=8 * pieces * part[1] * mode_rows * LANES, transcendentals=0
        ),
        compiler_params=pltpu.CompilerParams(vmem_limit_bytes=8 * 2**20),
        name="pack",
    )(me, pltpu.with_memory_space_constraint(field_slab, pltpu.HBM))


def gram_kernel(fibers, last, me, *refs):
    pieces = refs[:fibers]
    sum_in, high_out, low_out, high_ref, low_ref, sem, *sum_refs = refs[fibers:]
    blocks, mode_rows = pieces[0].shape[:2]
    mode = high_ref.shape[0]
    for place, piece in enumerate(pieces):
        source = lax.rem(me[0] + fibers - shift_of(place, fibers), fibers)
        rows = pl.ds(pl.multiple_of(source * mode_rows, mode_rows), mode_rows)
        for block in range(blocks):
            high, low = split(piece[block])
            columns = slice(block * LANES, (block + 1) * LANES)
            high_ref[rows, columns] = high
            low_ref[rows, columns] = low
    stores = [pltpu.make_async_copy(high_ref, high_out, sem.at[0]), pltpu.make_async_copy(low_ref, low_out, sem.at[1])]
    for store in stores:
        store.start()
    half = sum_in.shape[0] // 2
    place = 0
    step = 2 * LANES
    for top in range(0, mode, step):
        high, low = high_ref[top : top + step], low_ref[top : top + step]
        products = (
            contract_lanes(high, high_ref[top:])
            + contract_lanes(high, low_ref[top:])
            + contract_lanes(low, high_ref[top:])
        )
        for row in range(0, step, LANES):
            for column in range(row, mode - top, LANES):
                tile = sum_in[place : place + LANES] + products[row : row + LANES, column : column + LANES]
                if last:
                    index, offset = divmod(place, half)
                    sum_refs[0][lax.rem(me[1] + index, 2), offset : offset + LANES] = tile
                else:
                    sum_refs[0][place : place + LANES] = tile
                place += LANES
    if last:
        ordered, own_ref, other_ref = sum_refs
        own_ref[...] = ordered[0]
        other_ref[...] = ordered[1]
    for store in stores:
        store.wait()


def gram(me, pieces, running, last):
    fibers = len(pieces)
    blocks, mode_rows, _ = pieces[0].shape
    mode, columns = fibers * mode_rows, blocks * LANES
    half = jax.ShapeDtypeStruct((mode, columns), jnp.bfloat16)
    total, lanes = running.shape
    if last:
        sums = [jax.ShapeDtypeStruct((total // 2, lanes), jnp.float32)] * 2
        scratch, aliases = [pltpu.VMEM((2, total // 2, lanes), jnp.float32)], {}
    else:
        sums, scratch, aliases = [jax.ShapeDtypeStruct(running.shape, jnp.float32)], [], {fibers + 1: 2}

    def kernel(*refs):
        inputs, outputs = refs[: fibers + 4], refs[fibers + 4 :]
        results, buffers = outputs[: len(sums)], outputs[len(sums) :]
        gram_kernel(fibers, last, *inputs, *buffers, *results)

    return pl.pallas_call(
        kernel,
        out_shape=[pltpu.HBM(half.shape, half.dtype)] * 2 + sums,
        in_specs=[pl.BlockSpec(memory_space=pltpu.SMEM)] + [VMEM] * (fibers + 1),
        out_specs=[pl.BlockSpec(memory_space=pltpu.HBM)] * 2 + [VMEM] * len(sums),
        scratch_shapes=[pltpu.VMEM(half.shape, half.dtype)] * 2 + [pltpu.SemaphoreType.DMA((2,))] + scratch,
        input_output_aliases=aliases,
        cost_estimate=pl.CostEstimate(flops=6 * mode * mode * columns, bytes_accessed=8 * mode * columns, transcendentals=0),
        compiler_params=pltpu.CompilerParams(vmem_limit_bytes=16 * 2**20),
        name="gram",
    )(me, *pieces, running)


def dot(left, right, left_dim, right_dim):
    return lax.dot_general(
        left, right, (((left_dim,), (right_dim,)), ((), ())), precision=precise, preferred_element_type=jnp.float32
    )


def inverse_cholesky(inner, panel=32, block=16):
    rank = inner.shape[0]
    row = lax.broadcasted_iota(jnp.int32, (ROWS, rank), 0)
    rows = lax.broadcasted_iota(jnp.int32, (rank, rank), 0)
    lanes = lax.broadcasted_iota(jnp.int32, (rank, rank), 1)
    inverse = (rows == lanes).astype(jnp.float32)
    groups = panel // ROWS
    done = []
    for start in range(0, rank, panel):
        left = [inner[ROWS * i : ROWS * (i + 1)] for i in range(groups)]
        right = [inverse[ROWS * i : ROWS * (i + 1)] for i in range(groups)]
        for first in range(0, panel, block):
            columns = {}
            for i in range(first // ROWS, groups):
                for j in range(block):
                    column = left[i][:, start + first + j : start + first + j + 1]
                    columns[i, j] = jnp.broadcast_to(column, (ROWS, rank))
            for j in range(block):
                group, sub = divmod(first + j, ROWS)
                pivot_row = slice(sub, sub + 1)
                pivot = 1.0 / columns[group, j][pivot_row]
                heads = {k: columns[group, k][pivot_row] for k in range(j + 1, block)}
                left_row, right_row = left[group][pivot_row], right[group][pivot_row]
                for i in range(group, groups):
                    below = columns[i, j]
                    if i == group:
                        below = jnp.where(row > sub, below, 0.0)
                    scale = below * pivot
                    for k, head in heads.items():
                        change = (below * head) * pivot if k == j + 1 else scale * head
                        columns[i, k] = columns[i, k] - change
                    left[i] = left[i] - scale * left_row
                    right[i] = right[i] - scale * right_row
        top, bottom = jnp.concatenate(left, axis=0), jnp.concatenate(right, axis=0)
        diagonal = jnp.where(lanes[:panel] == rows[:panel] + start, top, 0.0)
        root = lax.rsqrt(jnp.sum(diagonal, axis=1, keepdims=True))
        top, bottom = top * root, bottom * root
        done.append(bottom)
        end = start + panel
        if end < rank:
            update = dot(top, jnp.concatenate([top, bottom], axis=1), 0, 0)
            inner = inner[panel:] - update[end:, :rank]
            inverse = inverse[panel:] - update[end:, rank:]
    return jnp.concatenate(done, axis=0)


def finish_kernel(parts, me, own_ref, other_ref, start_ref, *refs):
    count = len(parts)
    halves, (factor_ref, core_ref), refs = refs[: 2 * count], refs[2 * count : 2 * count + 2], refs[2 * count + 2 :]
    fields, refs = refs[: 2 * count], refs[2 * count :]
    results, (gram_ref, packed_ref, in_sem, out_sem) = refs[:count], refs[count:]
    loads = [pltpu.make_async_copy(half, field, in_sem.at[i]) for i, (half, field) in enumerate(zip(halves, fields))]
    for load in loads:
        load.start()
    packed_ref[me[1]] = own_ref[...]
    packed_ref[1 - me[1]] = other_ref[...]
    mode, rank = start_ref.shape
    half = own_ref.shape[0]
    place = 0
    for i in range(0, mode, LANES):
        for j in range(i, mode, LANES):
            index, offset = divmod(place, half)
            tile = packed_ref[index, offset : offset + LANES]
            gram_ref[i : i + LANES, j : j + LANES] = tile
            if j > i:
                gram_ref[j : j + LANES, i : i + LANES] = tile.T
            place += LANES
    basis = start_ref[...].T
    for iteration in range(ITERS):
        images = dot(basis, gram_ref[...], 1, 0)
        basis = dot(inverse_cholesky(dot(images, images, 1, 1)), images, 1, 0)
    factor_ref[...] = basis.T
    high, low = split(basis)
    both = jnp.concatenate([high, low], axis=0)
    stores = []
    for i, (start, blocks, lane_part) in enumerate(parts):
        loads[2 * i].wait()
        loads[2 * i + 1].wait()
        products = matmul(both, fields[2 * i][...])
        result = products[:rank] + products[rank:] + matmul(high, fields[2 * i + 1][...])
        for block in range(blocks):
            results[i][:, block, :] = result[:, block * LANES : (block + 1) * LANES]
        target = core_ref.at[:, pl.ds(start, blocks), pl.ds(lane_part * LANES, LANES)]
        stores.append(pltpu.make_async_copy(results[i], target, out_sem.at[i]))
        stores[-1].start()
    for store in stores:
        store.wait()


def finish(me, own, other, start_basis, halves, parts, blocks, width):
    mode, rank = start_basis.shape
    anywhere = pl.BlockSpec(memory_space=pltpu.HBM)
    return pl.pallas_call(
        functools.partial(finish_kernel, parts),
        out_shape=[
            jax.ShapeDtypeStruct((mode, rank), jnp.float32),
            jax.ShapeDtypeStruct((rank, blocks, width), jnp.float32),
        ],
        in_specs=[pl.BlockSpec(memory_space=pltpu.SMEM)] + [VMEM] * 3 + [anywhere] * len(halves),
        out_specs=[VMEM, anywhere],
        scratch_shapes=[pltpu.VMEM(half.shape, half.dtype) for half in halves]
        + [pltpu.VMEM((rank, part[1], LANES), jnp.float32) for part in parts]
        + [
            pltpu.VMEM((mode, mode), jnp.float32),
            pltpu.VMEM((2,) + own.shape, jnp.float32),
            pltpu.SemaphoreType.DMA((len(halves),)),
            pltpu.SemaphoreType.DMA((len(parts),)),
        ],
        compiler_params=pltpu.CompilerParams(vmem_limit_bytes=24 * 2**20),
        name="finish",
    )(me, own, other, start_basis, *[pltpu.with_memory_space_constraint(half, pltpu.HBM) for half in halves])


def column_parts(blocks, lane_parts):
    return [(start, ROWS, lane) for start in range(0, blocks, ROWS) for lane in range(lane_parts)]


def on_device(field_slab, start_basis):
    fiber = ("chip", "core")
    fibers, groups = lax.axis_size(fiber), lax.axis_size("group")
    mode_rows, blocks, width = field_slab.shape
    mode = fibers * mode_rows
    column_count = blocks * width * groups
    own_width = width // fibers
    me = jnp.stack([lax.axis_index(fiber), lax.axis_index("core")]).astype(jnp.int32)
    count = mode // LANES
    sums = [jnp.zeros((count * (count + 1) // 2 * LANES, LANES), jnp.float32)]
    halves = []
    parts = column_parts(blocks, own_width // LANES)
    for part in parts:
        if part == parts[0]:
            pieces = [*pack(field_slab, me, fibers, part, 0, 1), *pack(field_slab, me, fibers, part, 1, fibers)]
        else:
            pieces = [*pack(field_slab, me, fibers, part, 0, fibers)]
        for place in range(fibers - 1):
            shift = shift_of(place, fibers)
            ring = [(i, (i + shift) % fibers) for i in range(fibers)]
            pieces[place] = lax.ppermute(pieces[place], fiber, ring)
        high, low, *sums = gram(me, pieces, sums[0], part == parts[-1])
        halves += [high, low]
    own, other = sums
    own = own + lax.ppermute(other, "core", [(0, 1), (1, 0)])
    peers = ("chip", "group")
    members = lax.axis_size(peers)
    shares = lax.all_to_all(own.reshape(members, -1, LANES), peers, 0, 0)
    share = jnp.sum(shares, axis=0) / column_count
    own = lax.all_to_all(jnp.broadcast_to(share, (members,) + share.shape), peers, 0, 0).reshape(own.shape)
    other = lax.ppermute(own, "core", [(0, 1), (1, 0)])
    return tuple(finish(me, own, other, start_basis, halves, parts, blocks, own_width))


def solution(mesh):
    devices = mesh.devices.reshape(mesh.shape["fiber"] // 2, 2, mesh.shape["group"])
    return jax.shard_map(
        on_device,
        mesh=jax.sharding.Mesh(devices, ("chip", "core", "group")),
        in_specs=(P(("chip", "core"), "group", None), P()),
        out_specs=(P(), P(None, "group", ("chip", "core"))),
        check_vma=False,
    )
```

```python
import functools

import jax
import jax.numpy as jnp
from jax import lax
from jax.experimental import pallas as pl
from jax.experimental.pallas import tpu as pltpu
from jax.sharding import PartitionSpec as P

ITERS = 2
LANES = 128
ROWS = 8


precise = lax.Precision.HIGHEST
VMEM = pl.BlockSpec(memory_space=pltpu.VMEM)


def contract_lanes(left, right):
    return lax.dot_general(left, right, (((1,), (1,)), ((), ())), preferred_element_type=jnp.float32)


def matmul(left, right):
    return lax.dot_general(left, right, (((1,), (0,)), ((), ())), preferred_element_type=jnp.float32)


def split(values):
    high = values.astype(jnp.bfloat16)
    low = (values - high.astype(jnp.float32)).astype(jnp.bfloat16)
    return high, low


def shift_of(place, fibers):
    half = (place + 1) // 2
    return fibers // 2 + half - (place % 2) * 2 * half


def pack_kernel(fibers, part, first, me, field_ref, *refs):
    *piece_refs, loaded_ref, sem = refs
    start, count, lane_part = part
    own_width = field_ref.shape[2] // fibers
    loads = []
    for step in range(len(piece_refs)):
        target = lax.rem(me[0] + shift_of(step + first, fibers), fibers)
        lanes = pl.ds(pl.multiple_of(target * own_width + lane_part * LANES, LANES), LANES)
        source = field_ref.at[:, pl.ds(start // ROWS * ROWS, ROWS), lanes]
        loads.append(pltpu.make_async_copy(source, loaded_ref.at[step], sem.at[step]))
        loads[-1].start()
    for step, piece_ref in enumerate(piece_refs):
        loads[step].wait()
        for block in range(count):
            piece_ref[block] = loaded_ref[step, :, start % ROWS + block, :]


def pack(field_slab, me, fibers, part, first, last):
    mode_rows = field_slab.shape[0]
    piece = (part[1], mode_rows, LANES)
    pieces = last - first
    return pl.pallas_call(
        functools.partial(pack_kernel, fibers, part, first),
        out_shape=[jax.ShapeDtypeStruct(piece, jnp.float32)] * pieces,
        in_specs=[pl.BlockSpec(memory_space=pltpu.SMEM), pl.BlockSpec(memory_space=pltpu.HBM)],
        out_specs=[VMEM] * pieces,
        scratch_shapes=[
            pltpu.VMEM((pieces, mode_rows, ROWS, LANES), jnp.float32),
            pltpu.SemaphoreType.DMA((pieces,)),
        ],
        cost_estimate=pl.CostEstimate(
            flops=0, bytes_accessed=8 * pieces * part[1] * mode_rows * LANES, transcendentals=0
        ),
        compiler_params=pltpu.CompilerParams(vmem_limit_bytes=8 * 2**20),
        name="pack",
    )(me, pltpu.with_memory_space_constraint(field_slab, pltpu.HBM))


def gram_kernel(fibers, last, me, *refs):
    pieces = refs[:fibers]
    sum_in, high_out, low_out, high_ref, low_ref, sem, sum_ref = refs[fibers:]
    blocks, mode_rows = pieces[0].shape[:2]
    mode = high_ref.shape[0]
    own_rows = []
    for place in range(fibers):
        source = lax.rem(me[0] + fibers - shift_of(place, fibers), fibers)
        own_rows.append(pl.ds(pl.multiple_of(source * mode_rows, mode_rows), mode_rows))

    def stores(block):
        columns = pl.ds(pl.multiple_of(block * LANES, LANES), LANES)
        return [
            pltpu.make_async_copy(buffer.at[:, columns], out.at[:, columns], sem.at[i, block])
            for i, (buffer, out) in enumerate([(high_ref, high_out), (low_ref, low_out)])
        ]

    @pl.loop(0, blocks)
    def _(block):
        columns = pl.ds(pl.multiple_of(block * LANES, LANES), LANES)
        for rows, piece in zip(own_rows, pieces):
            high_ref[rows, columns], low_ref[rows, columns] = split(piece[block])
        for store in stores(block):
            store.start()

    half = sum_in.shape[0] // 2
    place = 0
    step = 2 * LANES
    for top in range(0, mode, step):
        high, low = high_ref[top : top + step], low_ref[top : top + step]
        products = (
            contract_lanes(high, high_ref[top:])
            + contract_lanes(high, low_ref[top:])
            + contract_lanes(low, high_ref[top:])
        )
        for row in range(0, step, LANES):
            for column in range(row, mode - top, LANES):
                tile = sum_in[place : place + LANES] + products[row : row + LANES, column : column + LANES]
                if last:
                    index, offset = divmod(place, half)
                    sum_ref[lax.rem(me[1] + index, 2), offset : offset + LANES] = tile
                else:
                    sum_ref[place : place + LANES] = tile
                place += LANES

    @pl.loop(0, blocks)
    def _(block):
        for store in stores(block):
            store.wait()


def gram(me, pieces, running, last):
    fibers = len(pieces)
    blocks, mode_rows, _ = pieces[0].shape
    mode, columns = fibers * mode_rows, blocks * LANES
    half = jax.ShapeDtypeStruct((mode, columns), jnp.bfloat16)
    total, lanes = running.shape
    if last:
        result, aliases = jax.ShapeDtypeStruct((2, total // 2, lanes), jnp.float32), {}
    else:
        result, aliases = jax.ShapeDtypeStruct(running.shape, jnp.float32), {fibers + 1: 2}

    def kernel(*refs):
        *inputs, sum_out, high_ref, low_ref, sem = refs
        gram_kernel(fibers, last, *inputs, high_ref, low_ref, sem, sum_out)

    return pl.pallas_call(
        kernel,
        out_shape=[pltpu.HBM(half.shape, half.dtype)] * 2 + [result],
        in_specs=[pl.BlockSpec(memory_space=pltpu.SMEM)] + [VMEM] * (fibers + 1),
        out_specs=[pl.BlockSpec(memory_space=pltpu.HBM)] * 2 + [VMEM],
        scratch_shapes=[pltpu.VMEM(half.shape, half.dtype)] * 2 + [pltpu.SemaphoreType.DMA((2, blocks))],
        input_output_aliases=aliases,
        cost_estimate=pl.CostEstimate(flops=6 * mode * mode * columns, bytes_accessed=8 * mode * columns, transcendentals=0),
        compiler_params=pltpu.CompilerParams(vmem_limit_bytes=16 * 2**20),
        name="gram",
    )(me, *pieces, running)


def dot(left, right, left_dim, right_dim):
    return lax.dot_general(
        left, right, (((left_dim,), (right_dim,)), ((), ())), precision=precise, preferred_element_type=jnp.float32
    )


def inverse_cholesky(inner, panel=64, block=16):
    rank = inner.shape[0]
    row = lax.broadcasted_iota(jnp.int32, (ROWS, rank), 0)
    rows = lax.broadcasted_iota(jnp.int32, (rank, rank), 0)
    lanes = lax.broadcasted_iota(jnp.int32, (rank, rank), 1)
    inverse = (rows == lanes).astype(jnp.float32)
    groups = panel // ROWS
    done = []
    for start in range(0, rank, panel):
        left = [inner[ROWS * i : ROWS * (i + 1)] for i in range(groups)]
        right = [inverse[ROWS * i : ROWS * (i + 1)] for i in range(groups)]
        for first in range(0, panel, block):
            columns = {}
            for i in range(first // ROWS, groups):
                for j in range(block):
                    column = left[i][:, start + first + j : start + first + j + 1]
                    columns[i, j] = jnp.broadcast_to(column, (ROWS, rank))
            for j in range(block):
                group, sub = divmod(first + j, ROWS)
                pivot_row = slice(sub, sub + 1)
                pivot = 1.0 / columns[group, j][pivot_row]
                heads = {k: columns[group, k][pivot_row] for k in range(j + 1, block)}
                left_row, right_row = left[group][pivot_row], right[group][pivot_row]
                for i in range(group, groups):
                    below = columns[i, j]
                    if i == group:
                        below = jnp.where(row > sub, below, 0.0)
                    scale = below * pivot
                    for k, head in heads.items():
                        change = (below * head) * pivot if k == j + 1 else scale * head
                        columns[i, k] = columns[i, k] - change
                    left[i] = left[i] - scale * left_row
                    right[i] = right[i] - scale * right_row
        top, bottom = jnp.concatenate(left, axis=0), jnp.concatenate(right, axis=0)
        diagonal = jnp.where(lanes[:panel] == rows[:panel] + start, top, 0.0)
        root = lax.rsqrt(jnp.sum(diagonal, axis=1, keepdims=True))
        top, bottom = top * root, bottom * root
        done.append(bottom)
        end = start + panel
        if end < rank:
            update = dot(top, jnp.concatenate([top, bottom], axis=1), 0, 0)
            inner = inner[panel:] - update[end:, :rank]
            inverse = inverse[panel:] - update[end:, rank:]
    return jnp.concatenate(done, axis=0)


def finish_kernel(parts, me, own_ref, other_ref, start_ref, *refs):
    count = len(parts)
    halves, (factor_ref, core_ref), refs = refs[: 2 * count], refs[2 * count : 2 * count + 2], refs[2 * count + 2 :]
    fields, refs = refs[: 2 * count], refs[2 * count :]
    results, (gram_ref, packed_ref, in_sem, out_sem) = refs[:count], refs[count:]
    loads = [pltpu.make_async_copy(half, field, in_sem.at[i]) for i, (half, field) in enumerate(zip(halves, fields))]
    for load in loads:
        load.start()
    mode, rank = start_ref.shape
    half = own_ref.shape[0]

    @pl.loop(0, half // (8 * ROWS))
    def _(i):
        rows = pl.ds(pl.multiple_of(i * 8 * ROWS, ROWS), 8 * ROWS)
        packed_ref[me[1], rows] = own_ref[rows]
        packed_ref[1 - me[1], rows] = other_ref[rows]

    place = 0
    for i in range(0, mode, LANES):
        for j in range(i, mode, LANES):
            index, offset = divmod(place, half)
            tile = packed_ref[index, offset : offset + LANES]
            gram_ref[i : i + LANES, j : j + LANES] = tile
            if j > i:
                gram_ref[j : j + LANES, i : i + LANES] = tile.T
            place += LANES
    basis = start_ref[...].T
    for iteration in range(ITERS):
        images = dot(basis, gram_ref[...], 1, 0)
        basis = dot(inverse_cholesky(dot(images, images, 1, 1)), images, 1, 0)
    factor_ref[...] = basis.T
    high, low = split(basis)
    both = jnp.concatenate([high, low], axis=0)
    stores = []
    for i, (start, blocks, lane_part) in enumerate(parts):
        loads[2 * i].wait()
        loads[2 * i + 1].wait()
        products = matmul(both, fields[2 * i][...])
        result = products[:rank] + products[rank:] + matmul(high, fields[2 * i + 1][...])
        for block in range(blocks):
            results[i][:, block, :] = result[:, block * LANES : (block + 1) * LANES]
        target = core_ref.at[:, pl.ds(start, blocks), pl.ds(lane_part * LANES, LANES)]
        stores.append(pltpu.make_async_copy(results[i], target, out_sem.at[i]))
        stores[-1].start()
    for store in stores:
        store.wait()


def finish(me, own, other, start_basis, halves, parts, blocks, width):
    mode, rank = start_basis.shape
    anywhere = pl.BlockSpec(memory_space=pltpu.HBM)
    return pl.pallas_call(
        functools.partial(finish_kernel, parts),
        out_shape=[
            jax.ShapeDtypeStruct((mode, rank), jnp.float32),
            jax.ShapeDtypeStruct((rank, blocks, width), jnp.float32),
        ],
        in_specs=[pl.BlockSpec(memory_space=pltpu.SMEM)] + [VMEM] * 3 + [anywhere] * len(halves),
        out_specs=[VMEM, anywhere],
        scratch_shapes=[pltpu.VMEM(half.shape, half.dtype) for half in halves]
        + [pltpu.VMEM((rank, part[1], LANES), jnp.float32) for part in parts]
        + [
            pltpu.VMEM((mode, mode), jnp.float32),
            pltpu.VMEM((2,) + own.shape, jnp.float32),
            pltpu.SemaphoreType.DMA((len(halves),)),
            pltpu.SemaphoreType.DMA((len(parts),)),
        ],
        compiler_params=pltpu.CompilerParams(vmem_limit_bytes=24 * 2**20),
        name="finish",
    )(me, own, other, start_basis, *[pltpu.with_memory_space_constraint(half, pltpu.HBM) for half in halves])


def column_parts(blocks, lane_parts):
    return [(start, ROWS, lane) for start in range(0, blocks, ROWS) for lane in range(lane_parts)]


def on_device(field_slab, start_basis):
    fiber = ("chip", "core")
    fibers, groups = lax.axis_size(fiber), lax.axis_size("group")
    mode_rows, blocks, width = field_slab.shape
    mode = fibers * mode_rows
    column_count = blocks * width * groups
    own_width = width // fibers
    me = jnp.stack([lax.axis_index(fiber), lax.axis_index("core")]).astype(jnp.int32)
    count = mode // LANES
    running = jnp.zeros((count * (count + 1) // 2 * LANES, LANES), jnp.float32)
    halves = []
    parts = column_parts(blocks, own_width // LANES)
    for part in parts:
        if part == parts[0]:
            pieces = [*pack(field_slab, me, fibers, part, 0, 1), *pack(field_slab, me, fibers, part, 1, fibers)]
        else:
            pieces = [*pack(field_slab, me, fibers, part, 0, fibers)]
        for place in range(fibers - 1):
            shift = shift_of(place, fibers)
            ring = [(i, (i + shift) % fibers) for i in range(fibers)]
            pieces[place] = lax.ppermute(pieces[place], fiber, ring)
        high, low, running = gram(me, pieces, running, part == parts[-1])
        halves += [high, low]
    own, other = running[0], running[1]
    own = own + lax.ppermute(other, "core", [(0, 1), (1, 0)])
    peers = ("chip", "group")
    members = lax.axis_size(peers)
    shares = lax.all_to_all(own.reshape(members, -1, LANES), peers, 0, 0)
    share = jnp.sum(shares, axis=0) / column_count
    own = lax.all_to_all(jnp.broadcast_to(share, (members,) + share.shape), peers, 0, 0).reshape(own.shape)
    other = lax.ppermute(own, "core", [(0, 1), (1, 0)])
    return tuple(finish(me, own, other, start_basis, halves, parts, blocks, own_width))


def solution(mesh):
    devices = mesh.devices.reshape(mesh.shape["fiber"] // 2, 2, mesh.shape["group"])
    return jax.shard_map(
        on_device,
        mesh=jax.sharding.Mesh(devices, ("chip", "core", "group")),
        in_specs=(P(("chip", "core"), "group", None), P()),
        out_specs=(P(), P(None, "group", ("chip", "core"))),
        check_vma=False,
    )
```

```python
import functools

import jax
import jax.numpy as jnp
from jax import lax
from jax.experimental import pallas as pl
from jax.experimental.pallas import tpu as pltpu
from jax.sharding import PartitionSpec as P

ITERS = 2
LANES = 128
ROWS = 8


precise = lax.Precision.HIGHEST
VMEM = pl.BlockSpec(memory_space=pltpu.VMEM)


def contract_lanes(left, right):
    return lax.dot_general(left, right, (((1,), (1,)), ((), ())), preferred_element_type=jnp.float32)


def matmul(left, right):
    return lax.dot_general(left, right, (((1,), (0,)), ((), ())), preferred_element_type=jnp.float32)


def split(values):
    high = values.astype(jnp.bfloat16)
    low = (values - high.astype(jnp.float32)).astype(jnp.bfloat16)
    return high, low


def shift_of(place, fibers):
    half = (place + 1) // 2
    return fibers // 2 + half - (place % 2) * 2 * half


def pack_kernel(fibers, part, first, me, field_ref, *refs):
    *piece_refs, loaded_ref, sem = refs
    start, count, lane_part = part
    own_width = field_ref.shape[2] // fibers
    loads = []
    for step in range(len(piece_refs)):
        target = lax.rem(me[0] + shift_of(step + first, fibers), fibers)
        lanes = pl.ds(pl.multiple_of(target * own_width + lane_part * LANES, LANES), LANES)
        source = field_ref.at[:, pl.ds(start // ROWS * ROWS, ROWS), lanes]
        loads.append(pltpu.make_async_copy(source, loaded_ref.at[step], sem.at[step]))
        loads[-1].start()
    for step, piece_ref in enumerate(piece_refs):
        loads[step].wait()
        for block in range(count):
            piece_ref[block] = loaded_ref[step, :, start % ROWS + block, :]


def pack(field_slab, me, fibers, part, first, last):
    mode_rows = field_slab.shape[0]
    piece = (part[1], mode_rows, LANES)
    pieces = last - first
    return pl.pallas_call(
        functools.partial(pack_kernel, fibers, part, first),
        out_shape=[jax.ShapeDtypeStruct(piece, jnp.float32)] * pieces,
        in_specs=[pl.BlockSpec(memory_space=pltpu.SMEM), pl.BlockSpec(memory_space=pltpu.HBM)],
        out_specs=[VMEM] * pieces,
        scratch_shapes=[
            pltpu.VMEM((pieces, mode_rows, ROWS, LANES), jnp.float32),
            pltpu.SemaphoreType.DMA((pieces,)),
        ],
        cost_estimate=pl.CostEstimate(
            flops=0, bytes_accessed=8 * pieces * part[1] * mode_rows * LANES, transcendentals=0
        ),
        compiler_params=pltpu.CompilerParams(vmem_limit_bytes=8 * 2**20),
        name="pack",
    )(me, pltpu.with_memory_space_constraint(field_slab, pltpu.HBM))


def gram_kernel(fibers, last, me, *refs):
    pieces = refs[:fibers]
    sum_in, high_out, low_out, high_ref, low_ref, sem, sum_ref = refs[fibers:]
    blocks, mode_rows = pieces[0].shape[:2]
    mode = high_ref.shape[0]
    for place, piece in enumerate(pieces):
        source = lax.rem(me[0] + fibers - shift_of(place, fibers), fibers)
        rows = pl.ds(pl.multiple_of(source * mode_rows, mode_rows), mode_rows)
        for block in range(blocks):
            columns = slice(block * LANES, (block + 1) * LANES)
            high_ref[rows, columns], low_ref[rows, columns] = split(piece[block])
    stores = [pltpu.make_async_copy(high_ref, high_out, sem.at[0]), pltpu.make_async_copy(low_ref, low_out, sem.at[1])]
    for store in stores:
        store.start()
    half = sum_in.shape[0] // 2
    place = 0
    step = 2 * LANES
    for top in range(0, mode, step):
        high, low = high_ref[top : top + step], low_ref[top : top + step]
        products = (
            contract_lanes(high, high_ref[top:])
            + contract_lanes(high, low_ref[top:])
            + contract_lanes(low, high_ref[top:])
        )
        for row in range(0, step, LANES):
            for column in range(row, mode - top, LANES):
                tile = sum_in[place : place + LANES] + products[row : row + LANES, column : column + LANES]
                if last:
                    index, offset = divmod(place, half)
                    sum_ref[lax.rem(me[1] + index, 2), offset : offset + LANES] = tile
                else:
                    sum_ref[place : place + LANES] = tile
                place += LANES

    for store in stores:
        store.wait()


def gram(me, pieces, running, last):
    fibers = len(pieces)
    blocks, mode_rows, _ = pieces[0].shape
    mode, columns = fibers * mode_rows, blocks * LANES
    half = jax.ShapeDtypeStruct((mode, columns), jnp.bfloat16)
    total, lanes = running.shape
    if last:
        result, aliases = jax.ShapeDtypeStruct((2, total // 2, lanes), jnp.float32), {}
    else:
        result, aliases = jax.ShapeDtypeStruct(running.shape, jnp.float32), {fibers + 1: 2}

    def kernel(*refs):
        *inputs, sum_out, high_ref, low_ref, sem = refs
        gram_kernel(fibers, last, *inputs, high_ref, low_ref, sem, sum_out)

    return pl.pallas_call(
        kernel,
        out_shape=[pltpu.HBM(half.shape, half.dtype)] * 2 + [result],
        in_specs=[pl.BlockSpec(memory_space=pltpu.SMEM)] + [VMEM] * (fibers + 1),
        out_specs=[pl.BlockSpec(memory_space=pltpu.HBM)] * 2 + [VMEM],
        scratch_shapes=[pltpu.VMEM(half.shape, half.dtype)] * 2 + [pltpu.SemaphoreType.DMA((2,))],
        input_output_aliases=aliases,
        cost_estimate=pl.CostEstimate(flops=6 * mode * mode * columns, bytes_accessed=8 * mode * columns, transcendentals=0),
        compiler_params=pltpu.CompilerParams(vmem_limit_bytes=16 * 2**20),
        name="gram",
    )(me, *pieces, running)


def dot(left, right, left_dim, right_dim):
    return lax.dot_general(
        left, right, (((left_dim,), (right_dim,)), ((), ())), precision=precise, preferred_element_type=jnp.float32
    )


def inverse_cholesky(inner, panel=64, block=16):
    rank = inner.shape[0]
    row = lax.broadcasted_iota(jnp.int32, (ROWS, rank), 0)
    rows = lax.broadcasted_iota(jnp.int32, (rank, rank), 0)
    lanes = lax.broadcasted_iota(jnp.int32, (rank, rank), 1)
    inverse = (rows == lanes).astype(jnp.float32)
    groups = panel // ROWS
    done = []
    for start in range(0, rank, panel):
        left = [inner[ROWS * i : ROWS * (i + 1)] for i in range(groups)]
        right = [inverse[ROWS * i : ROWS * (i + 1)] for i in range(groups)]
        for first in range(0, panel, block):
            columns = {}
            for i in range(first // ROWS, groups):
                for j in range(block):
                    column = left[i][:, start + first + j : start + first + j + 1]
                    columns[i, j] = jnp.broadcast_to(column, (ROWS, rank))
            for j in range(block):
                group, sub = divmod(first + j, ROWS)
                pivot_row = slice(sub, sub + 1)
                pivot = 1.0 / columns[group, j][pivot_row]
                heads = {k: columns[group, k][pivot_row] for k in range(j + 1, block)}
                left_row, right_row = left[group][pivot_row], right[group][pivot_row]
                for i in range(group, groups):
                    below = columns[i, j]
                    if i == group:
                        below = jnp.where(row > sub, below, 0.0)
                    scale = below * pivot
                    for k, head in heads.items():
                        change = (below * head) * pivot if k == j + 1 else scale * head
                        columns[i, k] = columns[i, k] - change
                    left[i] = left[i] - scale * left_row
                    right[i] = right[i] - scale * right_row
        top, bottom = jnp.concatenate(left, axis=0), jnp.concatenate(right, axis=0)
        diagonal = jnp.where(lanes[:panel] == rows[:panel] + start, top, 0.0)
        root = lax.rsqrt(jnp.sum(diagonal, axis=1, keepdims=True))
        top, bottom = top * root, bottom * root
        done.append(bottom)
        end = start + panel
        if end < rank:
            update = dot(top, jnp.concatenate([top, bottom], axis=1), 0, 0)
            inner = inner[panel:] - update[end:, :rank]
            inverse = inverse[panel:] - update[end:, rank:]
    return jnp.concatenate(done, axis=0)


def finish_kernel(parts, me, own_ref, other_ref, start_ref, *refs):
    count = len(parts)
    halves, (factor_ref, core_ref), refs = refs[: 2 * count], refs[2 * count : 2 * count + 2], refs[2 * count + 2 :]
    fields, refs = refs[: 2 * count], refs[2 * count :]
    results, (gram_ref, packed_ref, in_sem, out_sem) = refs[:count], refs[count:]
    loads = [pltpu.make_async_copy(half, field, in_sem.at[i]) for i, (half, field) in enumerate(zip(halves, fields))]
    for load in loads:
        load.start()
    mode, rank = start_ref.shape
    half = own_ref.shape[0]

    @pl.loop(0, half // (8 * ROWS))
    def _(i):
        rows = pl.ds(pl.multiple_of(i * 8 * ROWS, ROWS), 8 * ROWS)
        packed_ref[me[1], rows] = own_ref[rows]
        packed_ref[1 - me[1], rows] = other_ref[rows]

    place = 0
    for i in range(0, mode, LANES):
        for j in range(i, mode, LANES):
            index, offset = divmod(place, half)
            tile = packed_ref[index, offset : offset + LANES]
            gram_ref[i : i + LANES, j : j + LANES] = tile
            if j > i:
                gram_ref[j : j + LANES, i : i + LANES] = tile.T
            place += LANES
    basis = start_ref[...].T
    for iteration in range(ITERS):
        images = dot(basis, gram_ref[...], 1, 0)
        basis = dot(inverse_cholesky(dot(images, images, 1, 1)), images, 1, 0)
    factor_ref[...] = basis.T
    high, low = split(basis)
    both = jnp.concatenate([high, low], axis=0)
    stores = []
    for i, (start, blocks, lane_part) in enumerate(parts):
        loads[2 * i].wait()
        loads[2 * i + 1].wait()
        products = matmul(both, fields[2 * i][...])
        result = products[:rank] + products[rank:] + matmul(high, fields[2 * i + 1][...])
        for block in range(blocks):
            results[i][:, block, :] = result[:, block * LANES : (block + 1) * LANES]
        target = core_ref.at[:, pl.ds(start, blocks), pl.ds(lane_part * LANES, LANES)]
        stores.append(pltpu.make_async_copy(results[i], target, out_sem.at[i]))
        stores[-1].start()
    for store in stores:
        store.wait()


def finish(me, own, other, start_basis, halves, parts, blocks, width):
    mode, rank = start_basis.shape
    anywhere = pl.BlockSpec(memory_space=pltpu.HBM)
    return pl.pallas_call(
        functools.partial(finish_kernel, parts),
        out_shape=[
            jax.ShapeDtypeStruct((mode, rank), jnp.float32),
            jax.ShapeDtypeStruct((rank, blocks, width), jnp.float32),
        ],
        in_specs=[pl.BlockSpec(memory_space=pltpu.SMEM)] + [VMEM] * 3 + [anywhere] * len(halves),
        out_specs=[VMEM, anywhere],
        scratch_shapes=[pltpu.VMEM(half.shape, half.dtype) for half in halves]
        + [pltpu.VMEM((rank, part[1], LANES), jnp.float32) for part in parts]
        + [
            pltpu.VMEM((mode, mode), jnp.float32),
            pltpu.VMEM((2,) + own.shape, jnp.float32),
            pltpu.SemaphoreType.DMA((len(halves),)),
            pltpu.SemaphoreType.DMA((len(parts),)),
        ],
        compiler_params=pltpu.CompilerParams(vmem_limit_bytes=24 * 2**20),
        name="finish",
    )(me, own, other, start_basis, *[pltpu.with_memory_space_constraint(half, pltpu.HBM) for half in halves])


def column_parts(blocks, lane_parts):
    parts = [(start, ROWS, lane) for start in range(0, blocks, ROWS) for lane in range(lane_parts)]
    start, count, lane = parts.pop()
    return parts + [(start, count // 2, lane), (start + count // 2, count - count // 2, lane)]


def on_device(field_slab, start_basis):
    fiber = ("chip", "core")
    fibers, groups = lax.axis_size(fiber), lax.axis_size("group")
    mode_rows, blocks, width = field_slab.shape
    mode = fibers * mode_rows
    column_count = blocks * width * groups
    own_width = width // fibers
    me = jnp.stack([lax.axis_index(fiber), lax.axis_index("core")]).astype(jnp.int32)
    count = mode // LANES
    running = jnp.zeros((count * (count + 1) // 2 * LANES, LANES), jnp.float32)
    halves = []
    parts = column_parts(blocks, own_width // LANES)
    for part in parts:
        if part == parts[0]:
            pieces = [*pack(field_slab, me, fibers, part, 0, 1), *pack(field_slab, me, fibers, part, 1, fibers)]
        else:
            pieces = [*pack(field_slab, me, fibers, part, 0, fibers)]
        for place in range(fibers - 1):
            shift = shift_of(place, fibers)
            ring = [(i, (i + shift) % fibers) for i in range(fibers)]
            pieces[place] = lax.ppermute(pieces[place], fiber, ring)
        high, low, running = gram(me, pieces, running, part == parts[-1])
        halves += [high, low]
    own, other = running[0], running[1]
    own = own + lax.ppermute(other, "core", [(0, 1), (1, 0)])
    peers = ("chip", "group")
    members = lax.axis_size(peers)
    shares = lax.all_to_all(own.reshape(members, -1, LANES), peers, 0, 0)
    share = jnp.sum(shares, axis=0) / column_count
    own = lax.all_to_all(jnp.broadcast_to(share, (members,) + share.shape), peers, 0, 0).reshape(own.shape)
    other = lax.ppermute(own, "core", [(0, 1), (1, 0)])
    return tuple(finish(me, own, other, start_basis, halves, parts, blocks, own_width))


def solution(mesh):
    devices = mesh.devices.reshape(mesh.shape["fiber"] // 2, 2, mesh.shape["group"])
    return jax.shard_map(
        on_device,
        mesh=jax.sharding.Mesh(devices, ("chip", "core", "group")),
        in_specs=(P(("chip", "core"), "group", None), P()),
        out_specs=(P(), P(None, "group", ("chip", "core"))),
        check_vma=False,
    )
```

```python
import functools

import jax
import jax.numpy as jnp
from jax import lax
from jax.experimental import pallas as pl
from jax.experimental.pallas import tpu as pltpu
from jax.sharding import PartitionSpec as P

ITERS = 2
LANES = 128
ROWS = 8


precise = lax.Precision.HIGHEST
VMEM = pl.BlockSpec(memory_space=pltpu.VMEM)


def contract_lanes(left, right):
    return lax.dot_general(left, right, (((1,), (1,)), ((), ())), preferred_element_type=jnp.float32)


def matmul(left, right):
    return lax.dot_general(left, right, (((1,), (0,)), ((), ())), preferred_element_type=jnp.float32)


def split(values):
    high = values.astype(jnp.bfloat16)
    low = (values - high.astype(jnp.float32)).astype(jnp.bfloat16)
    return high, low


def shift_of(place, fibers):
    half = (place + 1) // 2
    return fibers // 2 + half - (place % 2) * 2 * half


def pack_kernel(fibers, part, first, me, field_ref, *refs):
    *piece_refs, loaded_ref, sem = refs
    start, count, lane_part = part
    own_width = field_ref.shape[2] // fibers
    loads = []
    for step in range(len(piece_refs)):
        target = lax.rem(me[0] + shift_of(step + first, fibers), fibers)
        lanes = pl.ds(pl.multiple_of(target * own_width + lane_part * LANES, LANES), LANES)
        source = field_ref.at[:, pl.ds(start // ROWS * ROWS, ROWS), lanes]
        loads.append(pltpu.make_async_copy(source, loaded_ref.at[step], sem.at[step]))
        loads[-1].start()
    for step, piece_ref in enumerate(piece_refs):
        loads[step].wait()
        for block in range(count):
            piece_ref[block] = loaded_ref[step, :, start % ROWS + block, :]


def pack(field_slab, me, fibers, part, first, last):
    mode_rows = field_slab.shape[0]
    piece = (part[1], mode_rows, LANES)
    pieces = last - first
    return pl.pallas_call(
        functools.partial(pack_kernel, fibers, part, first),
        out_shape=[jax.ShapeDtypeStruct(piece, jnp.float32)] * pieces,
        in_specs=[pl.BlockSpec(memory_space=pltpu.SMEM), pl.BlockSpec(memory_space=pltpu.HBM)],
        out_specs=[VMEM] * pieces,
        scratch_shapes=[
            pltpu.VMEM((pieces, mode_rows, ROWS, LANES), jnp.float32),
            pltpu.SemaphoreType.DMA((pieces,)),
        ],
        cost_estimate=pl.CostEstimate(
            flops=0, bytes_accessed=8 * pieces * part[1] * mode_rows * LANES, transcendentals=0
        ),
        compiler_params=pltpu.CompilerParams(vmem_limit_bytes=8 * 2**20),
        name="pack",
    )(me, pltpu.with_memory_space_constraint(field_slab, pltpu.HBM))


def gram_kernel(fibers, me, *refs):
    pieces = refs[:fibers]
    sum_in, high_out, low_out, high_ref, low_ref, sem, *sum_refs = refs[fibers:]
    blocks, mode_rows = pieces[0].shape[:2]
    mode = high_ref.shape[0]
    for place, piece in enumerate(pieces):
        source = lax.rem(me[0] + fibers - shift_of(place, fibers), fibers)
        rows = pl.ds(pl.multiple_of(source * mode_rows, mode_rows), mode_rows)
        for block in range(blocks):
            columns = slice(block * LANES, (block + 1) * LANES)
            high_ref[rows, columns], low_ref[rows, columns] = split(piece[block])
    stores = [pltpu.make_async_copy(high_ref, high_out, sem.at[0]), pltpu.make_async_copy(low_ref, low_out, sem.at[1])]
    for store in stores:
        store.start()
    place = 0
    step = 2 * LANES
    for top in range(0, mode, step):
        high, low = high_ref[top : top + step], low_ref[top : top + step]
        products = (
            contract_lanes(high, high_ref[top:])
            + contract_lanes(high, low_ref[top:])
            + contract_lanes(low, high_ref[top:])
        )
        for row in range(0, step, LANES):
            for column in range(row, mode - top, LANES):
                tile = products[row : row + LANES, column : column + LANES]
                sum_refs[0][place : place + LANES] = sum_in[place : place + LANES] + tile
                place += LANES

    if len(sum_refs) > 1:
        half = sum_in.shape[0] // 2
        for core in range(2):

            @pl.when(me[1] == core)
            def _():
                sum_refs[1 + core][...] = sum_refs[0][:half]
                sum_refs[2 - core][...] = sum_refs[0][half:]

    for store in stores:
        store.wait()


def gram(me, pieces, running, outputs):
    fibers = len(pieces)
    blocks, mode_rows, _ = pieces[0].shape
    mode, columns = fibers * mode_rows, blocks * LANES
    half = jax.ShapeDtypeStruct((mode, columns), jnp.bfloat16)
    total, lanes = running.shape

    def kernel(*refs):
        inputs, sums, (high_ref, low_ref, sem, *scratch) = refs[: fibers + 4], refs[fibers + 4 :][:outputs], refs[fibers + 4 :][outputs:]
        sums = (*scratch, *sums)
        gram_kernel(fibers, *inputs, high_ref, low_ref, sem, *sums)

    return pl.pallas_call(
        kernel,
        out_shape=[pltpu.HBM(half.shape, half.dtype)] * 2 + [jax.ShapeDtypeStruct((total // outputs, lanes), jnp.float32)] * outputs,
        in_specs=[pl.BlockSpec(memory_space=pltpu.SMEM)] + [VMEM] * (fibers + 1),
        out_specs=[pl.BlockSpec(memory_space=pltpu.HBM)] * 2 + [VMEM] * outputs,
        scratch_shapes=[pltpu.VMEM(half.shape, half.dtype)] * 2 + [pltpu.SemaphoreType.DMA((2,))] + [pltpu.VMEM(running.shape, jnp.float32)] * (outputs - 1),
        input_output_aliases={fibers + 1: 2} if outputs == 1 else {},
        cost_estimate=pl.CostEstimate(flops=6 * mode * mode * columns, bytes_accessed=8 * mode * columns, transcendentals=0),
        compiler_params=pltpu.CompilerParams(vmem_limit_bytes=16 * 2**20),
        name="gram",
    )(me, *pieces, running)


def dot(left, right, left_dim, right_dim):
    return lax.dot_general(
        left, right, (((left_dim,), (right_dim,)), ((), ())), precision=precise, preferred_element_type=jnp.float32
    )


def inverse_cholesky(inner, panel=64, block=16):
    rank = inner.shape[0]
    row = lax.broadcasted_iota(jnp.int32, (ROWS, rank), 0)
    rows = lax.broadcasted_iota(jnp.int32, (rank, rank), 0)
    lanes = lax.broadcasted_iota(jnp.int32, (rank, rank), 1)
    inverse = (rows == lanes).astype(jnp.float32)
    groups = panel // ROWS
    done = []
    for start in range(0, rank, panel):
        left = [inner[ROWS * i : ROWS * (i + 1)] for i in range(groups)]
        right = [inverse[ROWS * i : ROWS * (i + 1)] for i in range(groups)]
        for first in range(0, panel, block):
            columns = {}
            for i in range(first // ROWS, groups):
                for j in range(block):
                    column = left[i][:, start + first + j : start + first + j + 1]
                    columns[i, j] = jnp.broadcast_to(column, (ROWS, rank))
            for j in range(block):
                group, sub = divmod(first + j, ROWS)
                pivot_row = slice(sub, sub + 1)
                pivot = 1.0 / columns[group, j][pivot_row]
                heads = {k: columns[group, k][pivot_row] for k in range(j + 1, block)}
                left_row, right_row = left[group][pivot_row], right[group][pivot_row]
                for i in range(group, groups):
                    below = columns[i, j]
                    if i == group:
                        below = jnp.where(row > sub, below, 0.0)
                    scale = below * pivot
                    for k, head in heads.items():
                        change = (below * head) * pivot if k == j + 1 else scale * head
                        columns[i, k] = columns[i, k] - change
                    left[i] = left[i] - scale * left_row
                    right[i] = right[i] - scale * right_row
        top, bottom = jnp.concatenate(left, axis=0), jnp.concatenate(right, axis=0)
        diagonal = jnp.where(lanes[:panel] == rows[:panel] + start, top, 0.0)
        root = lax.rsqrt(jnp.sum(diagonal, axis=1, keepdims=True))
        top, bottom = top * root, bottom * root
        done.append(bottom)
        end = start + panel
        if end < rank:
            update = dot(top, jnp.concatenate([top, bottom], axis=1), 0, 0)
            inner = inner[panel:] - update[end:, :rank]
            inverse = inverse[panel:] - update[end:, rank:]
    return jnp.concatenate(done, axis=0)


def finish_kernel(parts, me, own_ref, other_ref, start_ref, *refs):
    count = len(parts)
    halves, (factor_ref, core_ref), refs = refs[: 2 * count], refs[2 * count : 2 * count + 2], refs[2 * count + 2 :]
    fields, refs = refs[: 2 * count], refs[2 * count :]
    results, (gram_ref, packed_ref, in_sem, out_sem) = refs[:count], refs[count:]
    loads = [pltpu.make_async_copy(half, field, in_sem.at[i]) for i, (half, field) in enumerate(zip(halves, fields))]
    for load in loads:
        load.start()
    mode, rank = start_ref.shape
    half = own_ref.shape[0]

    @pl.loop(0, half // (8 * ROWS))
    def _(i):
        rows = pl.ds(pl.multiple_of(i * 8 * ROWS, ROWS), 8 * ROWS)
        packed_ref[me[1], rows] = own_ref[rows]
        packed_ref[1 - me[1], rows] = other_ref[rows]

    place = 0
    for i in range(0, mode, LANES):
        for j in range(i, mode, LANES):
            index, offset = divmod(place, half)
            tile = packed_ref[index, offset : offset + LANES]
            gram_ref[i : i + LANES, j : j + LANES] = tile
            if j > i:
                gram_ref[j : j + LANES, i : i + LANES] = tile.T
            place += LANES
    basis = start_ref[...].T
    for iteration in range(ITERS):
        images = dot(basis, gram_ref[...], 1, 0)
        basis = dot(inverse_cholesky(dot(images, images, 1, 1)), images, 1, 0)
    factor_ref[...] = basis.T
    high, low = split(basis)
    both = jnp.concatenate([high, low], axis=0)
    stores = []
    for i, (start, blocks, lane_part) in enumerate(parts):
        loads[2 * i].wait()
        loads[2 * i + 1].wait()
        products = matmul(both, fields[2 * i][...])
        result = products[:rank] + products[rank:] + matmul(high, fields[2 * i + 1][...])
        for block in range(blocks):
            results[i][:, block, :] = result[:, block * LANES : (block + 1) * LANES]
        target = core_ref.at[:, pl.ds(start, blocks), pl.ds(lane_part * LANES, LANES)]
        stores.append(pltpu.make_async_copy(results[i], target, out_sem.at[i]))
        stores[-1].start()
    for store in stores:
        store.wait()


def finish(me, own, other, start_basis, halves, parts, blocks, width):
    mode, rank = start_basis.shape
    anywhere = pl.BlockSpec(memory_space=pltpu.HBM)
    return pl.pallas_call(
        functools.partial(finish_kernel, parts),
        out_shape=[
            jax.ShapeDtypeStruct((mode, rank), jnp.float32),
            jax.ShapeDtypeStruct((rank, blocks, width), jnp.float32),
        ],
        in_specs=[pl.BlockSpec(memory_space=pltpu.SMEM)] + [VMEM] * 3 + [anywhere] * len(halves),
        out_specs=[VMEM, anywhere],
        scratch_shapes=[pltpu.VMEM(half.shape, half.dtype) for half in halves]
        + [pltpu.VMEM((rank, part[1], LANES), jnp.float32) for part in parts]
        + [
            pltpu.VMEM((mode, mode), jnp.float32),
            pltpu.VMEM((2,) + own.shape, jnp.float32),
            pltpu.SemaphoreType.DMA((len(halves),)),
            pltpu.SemaphoreType.DMA((len(parts),)),
        ],
        compiler_params=pltpu.CompilerParams(vmem_limit_bytes=24 * 2**20),
        name="finish",
    )(me, own, other, start_basis, *[pltpu.with_memory_space_constraint(half, pltpu.HBM) for half in halves])


def column_parts(blocks, lane_parts):
    return [(start, ROWS, lane) for start in range(0, blocks, ROWS) for lane in range(lane_parts)]


def on_device(field_slab, start_basis):
    fiber = ("chip", "core")
    fibers, groups = lax.axis_size(fiber), lax.axis_size("group")
    mode_rows, blocks, width = field_slab.shape
    mode = fibers * mode_rows
    column_count = blocks * width * groups
    own_width = width // fibers
    me = jnp.stack([lax.axis_index(fiber), lax.axis_index("core")]).astype(jnp.int32)
    count = mode // LANES
    sums = [jnp.zeros((count * (count + 1) // 2 * LANES, LANES), jnp.float32)]
    halves = []
    parts = column_parts(blocks, own_width // LANES)
    for part in parts:
        if part == parts[0]:
            pieces = [*pack(field_slab, me, fibers, part, 0, 1), *pack(field_slab, me, fibers, part, 1, fibers)]
        else:
            pieces = [*pack(field_slab, me, fibers, part, 0, fibers)]
        for place in range(fibers - 1):
            shift = shift_of(place, fibers)
            ring = [(i, (i + shift) % fibers) for i in range(fibers)]
            pieces[place] = lax.ppermute(pieces[place], fiber, ring)
        high, low, *sums = gram(me, pieces, sums[0], 2 if part == parts[-1] else 1)
        halves += [high, low]
    own, other = sums
    own = own + lax.ppermute(other, "core", [(0, 1), (1, 0)])
    peers = ("chip", "group")
    members = lax.axis_size(peers)
    shares = lax.all_to_all(own.reshape(members, -1, LANES), peers, 0, 0)
    share = jnp.sum(shares, axis=0) / column_count
    own = lax.all_to_all(jnp.broadcast_to(share, (members,) + share.shape), peers, 0, 0).reshape(own.shape)
    other = lax.ppermute(own, "core", [(0, 1), (1, 0)])
    return tuple(finish(me, own, other, start_basis, halves, parts, blocks, own_width))


def solution(mesh):
    devices = mesh.devices.reshape(mesh.shape["fiber"] // 2, 2, mesh.shape["group"])
    return jax.shard_map(
        on_device,
        mesh=jax.sharding.Mesh(devices, ("chip", "core", "group")),
        in_specs=(P(("chip", "core"), "group", None), P()),
        out_specs=(P(), P(None, "group", ("chip", "core"))),
        check_vma=False,
    )
```

```python
import functools

import jax
import jax.numpy as jnp
from jax import lax
from jax.experimental import pallas as pl
from jax.experimental.pallas import tpu as pltpu
from jax.sharding import PartitionSpec as P

ITERS = 2
LANES = 128
ROWS = 8


precise = lax.Precision.HIGHEST
VMEM = pl.BlockSpec(memory_space=pltpu.VMEM)


def contract_lanes(left, right):
    return lax.dot_general(left, right, (((1,), (1,)), ((), ())), preferred_element_type=jnp.float32)


def matmul(left, right):
    return lax.dot_general(left, right, (((1,), (0,)), ((), ())), preferred_element_type=jnp.float32)


def split(values):
    high = values.astype(jnp.bfloat16)
    low = (values - high.astype(jnp.float32)).astype(jnp.bfloat16)
    return high, low


def shift_of(place, fibers):
    half = (place + 1) // 2
    return fibers // 2 + half - (place % 2) * 2 * half


def pack_kernel(fibers, part, first, me, field_ref, *refs):
    *piece_refs, loaded_ref, sem = refs
    start, count, lane_part = part
    own_width = field_ref.shape[2] // fibers
    loads = []
    for step in range(len(piece_refs)):
        target = lax.rem(me[0] + shift_of(step + first, fibers), fibers)
        lanes = pl.ds(pl.multiple_of(target * own_width + lane_part * LANES, LANES), LANES)
        source = field_ref.at[:, pl.ds(start // ROWS * ROWS, ROWS), lanes]
        loads.append(pltpu.make_async_copy(source, loaded_ref.at[step], sem.at[step]))
        loads[-1].start()
    for step, piece_ref in enumerate(piece_refs):
        loads[step].wait()
        for block in range(count):
            piece_ref[block] = loaded_ref[step, :, start % ROWS + block, :]


def pack(field_slab, me, fibers, part, first, last):
    mode_rows = field_slab.shape[0]
    piece = (part[1], mode_rows, LANES)
    pieces = last - first
    return pl.pallas_call(
        functools.partial(pack_kernel, fibers, part, first),
        out_shape=[jax.ShapeDtypeStruct(piece, jnp.float32)] * pieces,
        in_specs=[pl.BlockSpec(memory_space=pltpu.SMEM), pl.BlockSpec(memory_space=pltpu.HBM)],
        out_specs=[VMEM] * pieces,
        scratch_shapes=[
            pltpu.VMEM((pieces, mode_rows, ROWS, LANES), jnp.float32),
            pltpu.SemaphoreType.DMA((pieces,)),
        ],
        cost_estimate=pl.CostEstimate(
            flops=0, bytes_accessed=8 * pieces * part[1] * mode_rows * LANES, transcendentals=0
        ),
        compiler_params=pltpu.CompilerParams(vmem_limit_bytes=8 * 2**20),
        name="pack",
    )(me, pltpu.with_memory_space_constraint(field_slab, pltpu.HBM))


def gram_kernel(fibers, me, *refs):
    pieces = refs[:fibers]
    sum_in, high_out, low_out, high_ref, low_ref, sem, *sum_refs = refs[fibers:]
    blocks, mode_rows = pieces[0].shape[:2]
    mode = high_ref.shape[0]
    for place, piece in enumerate(pieces):
        source = lax.rem(me[0] + fibers - shift_of(place, fibers), fibers)
        rows = pl.ds(pl.multiple_of(source * mode_rows, mode_rows), mode_rows)
        for block in range(blocks):
            columns = slice(block * LANES, (block + 1) * LANES)
            high_ref[rows, columns], low_ref[rows, columns] = split(piece[block])
    stores = [pltpu.make_async_copy(high_ref, high_out, sem.at[0]), pltpu.make_async_copy(low_ref, low_out, sem.at[1])]
    for store in stores:
        store.start()
    place = 0
    step = 2 * LANES
    for top in range(0, mode, step):
        high, low = high_ref[top : top + step], low_ref[top : top + step]
        products = (
            contract_lanes(high, high_ref[top:])
            + contract_lanes(high, low_ref[top:])
            + contract_lanes(low, high_ref[top:])
        )
        for row in range(0, step, LANES):
            for column in range(row, mode - top, LANES):
                tile = products[row : row + LANES, column : column + LANES]
                sum_refs[0][place : place + LANES] = sum_in[place : place + LANES] + tile
                place += LANES

    if len(sum_refs) > 1:
        half = sum_in.shape[0] // 2
        for core in range(2):

            @pl.when(me[1] == core)
            def _():
                sum_refs[1 + core][...] = sum_refs[0][:half]
                sum_refs[2 - core][...] = sum_refs[0][half:]

    for store in stores:
        store.wait()


def gram(me, pieces, running, outputs):
    fibers = len(pieces)
    blocks, mode_rows, _ = pieces[0].shape
    mode, columns = fibers * mode_rows, blocks * LANES
    half = jax.ShapeDtypeStruct((mode, columns), jnp.bfloat16)
    total, lanes = running.shape

    def kernel(*refs):
        inputs, sums, (high_ref, low_ref, sem, *scratch) = refs[: fibers + 4], refs[fibers + 4 :][:outputs], refs[fibers + 4 :][outputs:]
        sums = (*scratch, *sums)
        gram_kernel(fibers, *inputs, high_ref, low_ref, sem, *sums)

    return pl.pallas_call(
        kernel,
        out_shape=[pltpu.HBM(half.shape, half.dtype)] * 2 + [jax.ShapeDtypeStruct((total // outputs, lanes), jnp.float32)] * outputs,
        in_specs=[pl.BlockSpec(memory_space=pltpu.SMEM)] + [VMEM] * (fibers + 1),
        out_specs=[pl.BlockSpec(memory_space=pltpu.HBM)] * 2 + [VMEM] * outputs,
        scratch_shapes=[pltpu.VMEM(half.shape, half.dtype)] * 2 + [pltpu.SemaphoreType.DMA((2,))] + [pltpu.VMEM(running.shape, jnp.float32)] * (outputs - 1),
        input_output_aliases={fibers + 1: 2} if outputs == 1 else {},
        cost_estimate=pl.CostEstimate(flops=6 * mode * mode * columns, bytes_accessed=8 * mode * columns, transcendentals=0),
        compiler_params=pltpu.CompilerParams(vmem_limit_bytes=16 * 2**20),
        name="gram",
    )(me, *pieces, running)


def dot(left, right, left_dim, right_dim):
    return lax.dot_general(
        left, right, (((left_dim,), (right_dim,)), ((), ())), precision=precise, preferred_element_type=jnp.float32
    )


def inverse_cholesky(inner, panel=64, block=16):
    rank = inner.shape[0]
    row = lax.broadcasted_iota(jnp.int32, (ROWS, rank), 0)
    rows = lax.broadcasted_iota(jnp.int32, (rank, rank), 0)
    lanes = lax.broadcasted_iota(jnp.int32, (rank, rank), 1)
    inverse = (rows == lanes).astype(jnp.float32)
    groups = panel // ROWS
    done = []
    for start in range(0, rank, panel):
        left = [inner[ROWS * i : ROWS * (i + 1)] for i in range(groups)]
        right = [inverse[ROWS * i : ROWS * (i + 1)] for i in range(groups)]
        for first in range(0, panel, block):
            columns = {}
            for i in range(first // ROWS, groups):
                for j in range(block):
                    column = left[i][:, start + first + j : start + first + j + 1]
                    columns[i, j] = jnp.broadcast_to(column, (ROWS, rank))
            for j in range(block):
                group, sub = divmod(first + j, ROWS)
                pivot_row = slice(sub, sub + 1)
                pivot = 1.0 / columns[group, j][pivot_row]
                heads = {k: columns[group, k][pivot_row] for k in range(j + 1, block)}
                left_row, right_row = left[group][pivot_row], right[group][pivot_row]
                for i in range(group, groups):
                    below = columns[i, j]
                    if i == group:
                        below = jnp.where(row > sub, below, 0.0)
                    scale = below * pivot
                    for k, head in heads.items():
                        change = (below * head) * pivot if k == j + 1 else scale * head
                        columns[i, k] = columns[i, k] - change
                    left[i] = left[i] - scale * left_row
                    right[i] = right[i] - scale * right_row
        top, bottom = jnp.concatenate(left, axis=0), jnp.concatenate(right, axis=0)
        diagonal = jnp.where(lanes[:panel] == rows[:panel] + start, top, 0.0)
        root = lax.rsqrt(jnp.sum(diagonal, axis=1, keepdims=True))
        top, bottom = top * root, bottom * root
        done.append(bottom)
        end = start + panel
        if end < rank:
            update = dot(top, jnp.concatenate([top, bottom], axis=1), 0, 0)
            inner = inner[panel:] - update[end:, :rank]
            inverse = inverse[panel:] - update[end:, rank:]
    return jnp.concatenate(done, axis=0)


def finish_kernel(parts, me, own_ref, other_ref, start_ref, *refs):
    count = len(parts)
    halves, (factor_ref, core_ref), refs = refs[: 2 * count], refs[2 * count : 2 * count + 2], refs[2 * count + 2 :]
    fields, refs = refs[: 2 * count], refs[2 * count :]
    results, (gram_ref, packed_ref, in_sem, out_sem) = refs[:count], refs[count:]
    loads = [pltpu.make_async_copy(half, field, in_sem.at[i]) for i, (half, field) in enumerate(zip(halves, fields))]
    for load in loads:
        load.start()
    mode, rank = start_ref.shape
    half = own_ref.shape[0]

    @pl.loop(0, half // (8 * ROWS))
    def _(i):
        rows = pl.ds(pl.multiple_of(i * 8 * ROWS, ROWS), 8 * ROWS)
        packed_ref[me[1], rows] = own_ref[rows]
        packed_ref[1 - me[1], rows] = other_ref[rows]

    place = 0
    for i in range(0, mode, LANES):
        for j in range(i, mode, LANES):
            index, offset = divmod(place, half)
            tile = packed_ref[index, offset : offset + LANES]
            gram_ref[i : i + LANES, j : j + LANES] = tile
            if j > i:
                gram_ref[j : j + LANES, i : i + LANES] = tile.T
            place += LANES
    basis = start_ref[...].T
    for iteration in range(ITERS):
        images = dot(basis, gram_ref[...], 1, 0)
        basis = dot(inverse_cholesky(dot(images, images, 1, 1)), images, 1, 0)
    factor_ref[...] = basis.T
    high, low = split(basis)
    both = jnp.concatenate([high, low], axis=0)
    stores = []
    for i, (start, blocks, lane_part) in enumerate(parts):
        loads[2 * i].wait()
        loads[2 * i + 1].wait()
        products = matmul(both, fields[2 * i][...])
        result = products[:rank] + products[rank:] + matmul(high, fields[2 * i + 1][...])
        for block in range(blocks):
            results[i][:, block, :] = result[:, block * LANES : (block + 1) * LANES]
        target = core_ref.at[:, pl.ds(start, blocks), pl.ds(lane_part * LANES, LANES)]
        stores.append(pltpu.make_async_copy(results[i], target, out_sem.at[i]))
        stores[-1].start()
    for store in stores:
        store.wait()


def finish(me, own, other, start_basis, halves, parts, blocks, width):
    mode, rank = start_basis.shape
    anywhere = pl.BlockSpec(memory_space=pltpu.HBM)
    return pl.pallas_call(
        functools.partial(finish_kernel, parts),
        out_shape=[
            jax.ShapeDtypeStruct((mode, rank), jnp.float32),
            jax.ShapeDtypeStruct((rank, blocks, width), jnp.float32),
        ],
        in_specs=[pl.BlockSpec(memory_space=pltpu.SMEM)] + [VMEM] * 3 + [anywhere] * len(halves),
        out_specs=[VMEM, anywhere],
        scratch_shapes=[pltpu.VMEM(half.shape, half.dtype) for half in halves]
        + [pltpu.VMEM((rank, part[1], LANES), jnp.float32) for part in parts]
        + [
            pltpu.VMEM((mode, mode), jnp.float32),
            pltpu.VMEM((2,) + own.shape, jnp.float32),
            pltpu.SemaphoreType.DMA((len(halves),)),
            pltpu.SemaphoreType.DMA((len(parts),)),
        ],
        compiler_params=pltpu.CompilerParams(vmem_limit_bytes=24 * 2**20),
        name="finish",
    )(me, own, other, start_basis, *[pltpu.with_memory_space_constraint(half, pltpu.HBM) for half in halves])


def column_parts(blocks, lane_parts):
    parts = [(start, ROWS, lane) for start in range(0, blocks, ROWS) for lane in range(lane_parts)]
    start, count, lane = parts.pop()
    return parts + [(start, count // 2, lane), (start + count // 2, count - count // 2, lane)]


def on_device(field_slab, start_basis):
    fiber = ("chip", "core")
    fibers, groups = lax.axis_size(fiber), lax.axis_size("group")
    mode_rows, blocks, width = field_slab.shape
    mode = fibers * mode_rows
    column_count = blocks * width * groups
    own_width = width // fibers
    me = jnp.stack([lax.axis_index(fiber), lax.axis_index("core")]).astype(jnp.int32)
    count = mode // LANES
    sums = [jnp.zeros((count * (count + 1) // 2 * LANES, LANES), jnp.float32)]
    halves = []
    parts = column_parts(blocks, own_width // LANES)
    for part in parts:
        if part == parts[0]:
            early = fibers // 2 + 1
            pieces = [*pack(field_slab, me, fibers, part, 0, early), *pack(field_slab, me, fibers, part, early, fibers)]
        else:
            pieces = [*pack(field_slab, me, fibers, part, 0, fibers)]
        for place in range(fibers - 1):
            shift = shift_of(place, fibers)
            ring = [(i, (i + shift) % fibers) for i in range(fibers)]
            pieces[place] = lax.ppermute(pieces[place], fiber, ring)
        high, low, *sums = gram(me, pieces, sums[0], 2 if part == parts[-1] else 1)
        halves += [high, low]
    own, other = sums
    own = own + lax.ppermute(other, "core", [(0, 1), (1, 0)])
    peers = ("chip", "group")
    members = lax.axis_size(peers)
    shares = lax.all_to_all(own.reshape(members, -1, LANES), peers, 0, 0)
    share = jnp.sum(shares, axis=0) / column_count
    own = lax.all_to_all(jnp.broadcast_to(share, (members,) + share.shape), peers, 0, 0).reshape(own.shape)
    other = lax.ppermute(own, "core", [(0, 1), (1, 0)])
    return tuple(finish(me, own, other, start_basis, halves, parts, blocks, own_width))


def solution(mesh):
    devices = mesh.devices.reshape(mesh.shape["fiber"] // 2, 2, mesh.shape["group"])
    return jax.shard_map(
        on_device,
        mesh=jax.sharding.Mesh(devices, ("chip", "core", "group")),
        in_specs=(P(("chip", "core"), "group", None), P()),
        out_specs=(P(), P(None, "group", ("chip", "core"))),
        check_vma=False,
    )
```

```python
import functools

import jax
import jax.numpy as jnp
from jax import lax
from jax.experimental import pallas as pl
from jax.experimental.pallas import tpu as pltpu
from jax.sharding import PartitionSpec as P

ITERS = 2
LANES = 128
ROWS = 8


precise = lax.Precision.HIGHEST
VMEM = pl.BlockSpec(memory_space=pltpu.VMEM)


def contract_lanes(left, right):
    return lax.dot_general(left, right, (((1,), (1,)), ((), ())), preferred_element_type=jnp.float32)


def matmul(left, right):
    return lax.dot_general(left, right, (((1,), (0,)), ((), ())), preferred_element_type=jnp.float32)


def split(values):
    high = values.astype(jnp.bfloat16)
    low = (values - high.astype(jnp.float32)).astype(jnp.bfloat16)
    return high, low


def shift_of(place, fibers):
    half = (place + 1) // 2
    return fibers // 2 + half - (place % 2) * 2 * half


def pack_kernel(fibers, part, first, me, field_ref, *refs):
    *piece_refs, loaded_ref, sem = refs
    start, count, lane_part = part
    own_width = field_ref.shape[2] // fibers
    loads = []
    for step in range(len(piece_refs)):
        target = lax.rem(me[0] + shift_of(step + first, fibers), fibers)
        lanes = pl.ds(pl.multiple_of(target * own_width + lane_part * LANES, LANES), LANES)
        source = field_ref.at[:, pl.ds(start // ROWS * ROWS, ROWS), lanes]
        loads.append(pltpu.make_async_copy(source, loaded_ref.at[step], sem.at[step]))
        loads[-1].start()
    for step, piece_ref in enumerate(piece_refs):
        loads[step].wait()
        for block in range(count):
            piece_ref[block] = loaded_ref[step, :, start % ROWS + block, :]


def pack(field_slab, me, fibers, part, first, last):
    mode_rows = field_slab.shape[0]
    piece = (part[1], mode_rows, LANES)
    pieces = last - first
    return pl.pallas_call(
        functools.partial(pack_kernel, fibers, part, first),
        out_shape=[jax.ShapeDtypeStruct(piece, jnp.float32)] * pieces,
        in_specs=[pl.BlockSpec(memory_space=pltpu.SMEM), pl.BlockSpec(memory_space=pltpu.HBM)],
        out_specs=[VMEM] * pieces,
        scratch_shapes=[
            pltpu.VMEM((pieces, mode_rows, ROWS, LANES), jnp.float32),
            pltpu.SemaphoreType.DMA((pieces,)),
        ],
        cost_estimate=pl.CostEstimate(
            flops=0, bytes_accessed=8 * pieces * part[1] * mode_rows * LANES, transcendentals=0
        ),
        compiler_params=pltpu.CompilerParams(vmem_limit_bytes=8 * 2**20),
        name="pack",
    )(me, pltpu.with_memory_space_constraint(field_slab, pltpu.HBM))


def gram_kernel(fibers, me, *refs):
    pieces = refs[:fibers]
    sum_in, high_out, low_out, high_ref, low_ref, sem, *sum_refs = refs[fibers:]
    blocks, mode_rows = pieces[0].shape[:2]
    mode = high_ref.shape[0]
    for place, piece in enumerate(pieces):
        source = lax.rem(me[0] + fibers - shift_of(place, fibers), fibers)
        rows = pl.ds(pl.multiple_of(source * mode_rows, mode_rows), mode_rows)
        for block in range(blocks):
            columns = slice(block * LANES, (block + 1) * LANES)
            high_ref[rows, columns], low_ref[rows, columns] = split(piece[block])
    stores = [pltpu.make_async_copy(high_ref, high_out, sem.at[0]), pltpu.make_async_copy(low_ref, low_out, sem.at[1])]
    for store in stores:
        store.start()
    place = 0
    step = 2 * LANES
    for top in range(0, mode, step):
        high, low = high_ref[top : top + step], low_ref[top : top + step]
        products = (
            contract_lanes(high, high_ref[top:])
            + contract_lanes(high, low_ref[top:])
            + contract_lanes(low, high_ref[top:])
        )
        for row in range(0, step, LANES):
            for column in range(row, mode - top, LANES):
                tile = products[row : row + LANES, column : column + LANES]
                sum_refs[0][place : place + LANES] = sum_in[place : place + LANES] + tile
                place += LANES

    if len(sum_refs) > 1:
        half = sum_in.shape[0] // 2
        for core in range(2):

            @pl.when(me[1] == core)
            def _():
                sum_refs[1 + core][...] = sum_refs[0][:half]
                sum_refs[2 - core][...] = sum_refs[0][half:]

    for store in stores:
        store.wait()


def gram(me, pieces, running, outputs):
    fibers = len(pieces)
    blocks, mode_rows, _ = pieces[0].shape
    mode, columns = fibers * mode_rows, blocks * LANES
    half = jax.ShapeDtypeStruct((mode, columns), jnp.bfloat16)
    total, lanes = running.shape

    def kernel(*refs):
        inputs, sums, (high_ref, low_ref, sem, *scratch) = refs[: fibers + 4], refs[fibers + 4 :][:outputs], refs[fibers + 4 :][outputs:]
        sums = (*scratch, *sums)
        gram_kernel(fibers, *inputs, high_ref, low_ref, sem, *sums)

    return pl.pallas_call(
        kernel,
        out_shape=[pltpu.HBM(half.shape, half.dtype)] * 2 + [jax.ShapeDtypeStruct((total // outputs, lanes), jnp.float32)] * outputs,
        in_specs=[pl.BlockSpec(memory_space=pltpu.SMEM)] + [VMEM] * (fibers + 1),
        out_specs=[pl.BlockSpec(memory_space=pltpu.HBM)] * 2 + [VMEM] * outputs,
        scratch_shapes=[pltpu.VMEM(half.shape, half.dtype)] * 2 + [pltpu.SemaphoreType.DMA((2,))] + [pltpu.VMEM(running.shape, jnp.float32)] * (outputs - 1),
        input_output_aliases={fibers + 1: 2} if outputs == 1 else {},
        cost_estimate=pl.CostEstimate(flops=6 * mode * mode * columns, bytes_accessed=8 * mode * columns, transcendentals=0),
        compiler_params=pltpu.CompilerParams(vmem_limit_bytes=16 * 2**20),
        name="gram",
    )(me, *pieces, running)


def dot(left, right, left_dim, right_dim):
    return lax.dot_general(
        left, right, (((left_dim,), (right_dim,)), ((), ())), precision=precise, preferred_element_type=jnp.float32
    )


def inverse_cholesky(inner, panel=64, block=16):
    rank = inner.shape[0]
    row = lax.broadcasted_iota(jnp.int32, (ROWS, rank), 0)
    rows = lax.broadcasted_iota(jnp.int32, (rank, rank), 0)
    lanes = lax.broadcasted_iota(jnp.int32, (rank, rank), 1)
    inverse = (rows == lanes).astype(jnp.float32)
    groups = panel // ROWS
    done = []
    for start in range(0, rank, panel):
        left = [inner[ROWS * i : ROWS * (i + 1)] for i in range(groups)]
        right = [inverse[ROWS * i : ROWS * (i + 1)] for i in range(groups)]
        for first in range(0, panel, block):
            columns = {}
            for i in range(first // ROWS, groups):
                for j in range(block):
                    column = left[i][:, start + first + j : start + first + j + 1]
                    columns[i, j] = jnp.broadcast_to(column, (ROWS, rank))
            for j in range(block):
                group, sub = divmod(first + j, ROWS)
                pivot_row = slice(sub, sub + 1)
                pivot = 1.0 / columns[group, j][pivot_row]
                heads = {k: columns[group, k][pivot_row] for k in range(j + 1, block)}
                left_row, right_row = left[group][pivot_row], right[group][pivot_row]
                for i in range(group, groups):
                    below = columns[i, j]
                    if i == group:
                        below = jnp.where(row > sub, below, 0.0)
                    scale = below * pivot
                    for k, head in heads.items():
                        change = (below * head) * pivot if k == j + 1 else scale * head
                        columns[i, k] = columns[i, k] - change
                    left[i] = left[i] - scale * left_row
                    right[i] = right[i] - scale * right_row
        top, bottom = jnp.concatenate(left, axis=0), jnp.concatenate(right, axis=0)
        diagonal = jnp.where(lanes[:panel] == rows[:panel] + start, top, 0.0)
        root = lax.rsqrt(jnp.sum(diagonal, axis=1, keepdims=True))
        top, bottom = top * root, bottom * root
        done.append(bottom)
        end = start + panel
        if end < rank:
            update = dot(top, jnp.concatenate([top, bottom], axis=1), 0, 0)
            inner = inner[panel:] - update[end:, :rank]
            inverse = inverse[panel:] - update[end:, rank:]
    return jnp.concatenate(done, axis=0)


def finish_kernel(parts, me, own_ref, other_ref, start_ref, *refs):
    count = len(parts)
    halves, (factor_ref, core_ref), refs = refs[: 2 * count], refs[2 * count : 2 * count + 2], refs[2 * count + 2 :]
    fields, refs = refs[: 2 * count], refs[2 * count :]
    results, (gram_ref, packed_ref, in_sem, out_sem) = refs[:count], refs[count:]
    loads = [pltpu.make_async_copy(half, field, in_sem.at[i]) for i, (half, field) in enumerate(zip(halves, fields))]
    for load in loads:
        load.start()
    mode, rank = start_ref.shape
    half = own_ref.shape[0]

    @pl.loop(0, half // LANES)
    def _(i):
        rows = pl.ds(pl.multiple_of(i * LANES, LANES), LANES)
        packed_ref[me[1], rows] = own_ref[rows]
        packed_ref[1 - me[1], rows] = other_ref[rows]

    place = 0
    for i in range(0, mode, LANES):
        for j in range(i, mode, LANES):
            index, offset = divmod(place, half)
            tile = packed_ref[index, offset : offset + LANES]
            gram_ref[i : i + LANES, j : j + LANES] = tile
            if j > i:
                gram_ref[j : j + LANES, i : i + LANES] = tile.T
            place += LANES
    basis = start_ref[...].T
    for iteration in range(ITERS):
        images = dot(basis, gram_ref[...], 1, 0)
        basis = dot(inverse_cholesky(dot(images, images, 1, 1)), images, 1, 0)
    factor_ref[...] = basis.T
    high, low = split(basis)
    both = jnp.concatenate([high, low], axis=0)
    stores = []
    for i, (start, blocks, lane_part) in enumerate(parts):
        loads[2 * i].wait()
        loads[2 * i + 1].wait()
        products = matmul(both, fields[2 * i][...])
        result = products[:rank] + products[rank:] + matmul(high, fields[2 * i + 1][...])
        for block in range(blocks):
            results[i][:, block, :] = result[:, block * LANES : (block + 1) * LANES]
        target = core_ref.at[:, pl.ds(start, blocks), pl.ds(lane_part * LANES, LANES)]
        stores.append(pltpu.make_async_copy(results[i], target, out_sem.at[i]))
        stores[-1].start()
    for store in stores:
        store.wait()


def finish(me, own, other, start_basis, halves, parts, blocks, width):
    mode, rank = start_basis.shape
    anywhere = pl.BlockSpec(memory_space=pltpu.HBM)
    return pl.pallas_call(
        functools.partial(finish_kernel, parts),
        out_shape=[
            jax.ShapeDtypeStruct((mode, rank), jnp.float32),
            jax.ShapeDtypeStruct((rank, blocks, width), jnp.float32),
        ],
        in_specs=[pl.BlockSpec(memory_space=pltpu.SMEM)] + [VMEM] * 3 + [anywhere] * len(halves),
        out_specs=[VMEM, anywhere],
        scratch_shapes=[pltpu.VMEM(half.shape, half.dtype) for half in halves]
        + [pltpu.VMEM((rank, part[1], LANES), jnp.float32) for part in parts]
        + [
            pltpu.VMEM((mode, mode), jnp.float32),
            pltpu.VMEM((2,) + own.shape, jnp.float32),
            pltpu.SemaphoreType.DMA((len(halves),)),
            pltpu.SemaphoreType.DMA((len(parts),)),
        ],
        compiler_params=pltpu.CompilerParams(vmem_limit_bytes=24 * 2**20),
        name="finish",
    )(me, own, other, start_basis, *[pltpu.with_memory_space_constraint(half, pltpu.HBM) for half in halves])


def column_parts(blocks, lane_parts):
    return [(start, ROWS, lane) for start in range(0, blocks, ROWS) for lane in range(lane_parts)]


def on_device(field_slab, start_basis):
    fiber = ("chip", "core")
    fibers, groups = lax.axis_size(fiber), lax.axis_size("group")
    mode_rows, blocks, width = field_slab.shape
    mode = fibers * mode_rows
    column_count = blocks * width * groups
    own_width = width // fibers
    me = jnp.stack([lax.axis_index(fiber), lax.axis_index("core")]).astype(jnp.int32)
    count = mode // LANES
    sums = [jnp.zeros((count * (count + 1) // 2 * LANES, LANES), jnp.float32)]
    halves = []
    parts = column_parts(blocks, own_width // LANES)
    for part in parts:
        if part == parts[0]:
            pieces = [*pack(field_slab, me, fibers, part, 0, 1), *pack(field_slab, me, fibers, part, 1, fibers)]
        else:
            pieces = [*pack(field_slab, me, fibers, part, 0, fibers)]
        for place in range(fibers - 1):
            shift = shift_of(place, fibers)
            ring = [(i, (i + shift) % fibers) for i in range(fibers)]
            pieces[place] = lax.ppermute(pieces[place], fiber, ring)
        high, low, *sums = gram(me, pieces, sums[0], 2 if part == parts[-1] else 1)
        halves += [high, low]
    own, other = sums
    own = own + lax.ppermute(other, "core", [(0, 1), (1, 0)])
    peers = ("chip", "group")
    members = lax.axis_size(peers)
    shares = lax.all_to_all(own.reshape(members, -1, LANES), peers, 0, 0)
    share = jnp.sum(shares, axis=0) / column_count
    own = lax.all_to_all(jnp.broadcast_to(share, (members,) + share.shape), peers, 0, 0).reshape(own.shape)
    other = lax.ppermute(own, "core", [(0, 1), (1, 0)])
    return tuple(finish(me, own, other, start_basis, halves, parts, blocks, own_width))


def solution(mesh):
    devices = mesh.devices.reshape(mesh.shape["fiber"] // 2, 2, mesh.shape["group"])
    return jax.shard_map(
        on_device,
        mesh=jax.sharding.Mesh(devices, ("chip", "core", "group")),
        in_specs=(P(("chip", "core"), "group", None), P()),
        out_specs=(P(), P(None, "group", ("chip", "core"))),
        check_vma=False,
    )
```
